256 devices in a mesh: cls: 8 (over z), col: 32 (over y, x, core).
Axes of the slice: x: 4, y: 4, z: 8, core: 2. Of those that a mesh axis runs over, the one named last changes fastest.
Arguments:
- coeffs_t: float32 [49152, 1024], P(('cls', 'col')), may hold values from -6 to 6
- alpha_table: float32 [64, 4096], replicated, may hold values from -0.1875 to 0.1875
- alpha_blocks: int32 [16, 16], replicated, may hold values from 0 to 15, all different within a row
- alpha_types: int32 [16, 16], replicated, may hold values from 0 to 63
- beta_table: float32 [64, 4096], replicated, may hold values from -0.21875 to 0.21875
- beta_blocks: int32 [768, 12], P('cls'), may hold values from 0 to 191, all different within a row
- beta_types: int32 [768, 12], P('cls'), may hold values from 0 to 63
- row_counts: int32 [32], replicated, may hold values from 1 to 48, 1024 in all
Outputs:
- sigma_slots: float32 [1536, 49152], P('col', 'cls')
The draws below stay inside these ranges and needn't reach their ends.
Inputs may be any that keep to these rules, and one draw needn't show every extreme that they name: `alpha_blocks`: each row names 16 different alpha blocks. `beta_blocks`: each row names 12 different entries: below 96 a block of the own class, from 96 on a block of the partner class. `row_counts`: the counts sum to 1024 and the largest is exactly 48.
All inputs are finite; a program needn't handle non-finite values.
Results may differ from the reference program's by a relative error of at most 0.0003.
Values sent between devices are 32-bit elements; how exact they have to be, the bound alone decides.
No kernel may reach another device: no remote copies, remote signals or barrier semaphores. Data moves between devices by JAX's collectives and lax.ppermute only.
A program may use at most 64 MiB of HBM per device.

```python
import math
import jax
import jax.numpy as jnp
import numpy as np
from jax import lax

NA = 1024
NB = 49152
BLOCK = 64
ALPHA_K = 16
BETA_K = 12
TYPES = 64
NAB = 16
NBB = 768
NBC = 96
CAP = 48
N_CLS = 8
N_COL = 32


def place_ends(array, own_key, least, top_value):
    index_at = [jax.random.randint(jax.random.fold_in(own_key, axis), (), 0, length) for axis, length in enumerate(array.shape)]
    widest = array.shape.index(max(array.shape))
    beside = index_at[:widest] + [(index_at[widest] + 1) % array.shape[widest]] + index_at[widest + 1:]
    return array.at[tuple(index_at)].set(least).at[tuple(beside)].set(top_value)


def block_levels(own_key, dims, shards, least, top_value):
    def one(dim, parts):
        steps = jax.random.uniform(jax.random.fold_in(jax.random.fold_in(own_key, 6), dim), (parts,), jnp.float32, least / len(shards), top_value / len(shards))
        return jnp.repeat(jnp.exp(steps), dims[dim] // parts).reshape((-1,) + (1,) * (len(dims) - dim - 1))

    gain = one(*shards[0])
    for cut in shards[1:]:
        gain = gain * one(*cut)
    return gain


def different_ones(rng, rows, number_of, top, lift):
    sequence = jax.random.permutation(jax.random.fold_in(rng, 1), number_of)
    favour = sequence
    for power in range(3):
        favour = favour * favour // number_of
    favour = favour * lift // number_of
    chance = jax.random.randint(jax.random.fold_in(rng, 2), (rows, number_of), 0, 4096) + favour
    holders = jax.random.permutation(jax.random.fold_in(rng, 3), rows)[jnp.arange(number_of) % rows]
    chance = jnp.where(jnp.arange(rows)[:, None] == holders[None, :], 1 << 14, chance)
    priority = chance * number_of + jnp.arange(number_of)
    return lax.top_k(priority.astype(jnp.int32), top)[1].astype(jnp.int32)


def length_profile(number_of, total, reach, slope):
    loads = [(1 << 20) // math.isqrt(rank ** slope) + 1 for rank in range(2, number_of + 1)]
    spare, holding = total - reach - (number_of - 1), [1] * (number_of - 1)
    while spare > 0:
        movable = [i for i in range(number_of - 1) if holding[i] < reach]
        whole, budget = sum([loads[i] for i in movable]), spare
        for i in movable:
            more = min(reach - holding[i], max(1, budget * loads[i] // whole), spare)
            holding[i] = holding[i] + more
            spare = spare - more
    return np.array([reach] + holding)


def ragged_sizes(stream_key, count, total, reach, lean):
    if count == 2:
        one = jax.random.randint(stream_key, (), max(1, total - reach), min(reach, total - 1) + 1)
        return jnp.stack([one, total - one])
    sizes = jnp.asarray(length_profile(count, total, reach, lean), jnp.int32)
    pairs = (count - 1) // 2
    source_of, taker = sizes[1:1 + 2 * pairs:2], sizes[2:2 + 2 * pairs:2]
    slack = jnp.minimum(source_of - 1, reach - taker)
    moved = jax.random.randint(jax.random.fold_in(stream_key, 1), (pairs,), 0, 1 << 20) % (slack + 1)
    sizes = sizes.at[1:1 + 2 * pairs:2].set(source_of - moved).at[2:2 + 2 * pairs:2].set(taker + moved)
    return sizes[jax.random.permutation(jax.random.fold_in(stream_key, 2), count)]


def bell_draw(rng, extent, spread, bound, split=(), kind=jnp.bfloat16):
    gain = block_levels(rng, extent, split, -0.22, 0.18) if split else 1.0
    result = jax.random.normal(rng, extent, jnp.float32) * spread * gain
    return jnp.minimum(jnp.maximum(result, -bound), bound).astype(kind)


def setup_inputs(seed: int = 0) -> dict:
    key_of = jax.random.split(jax.random.key(seed), 9)
    coeffs_t = bell_draw(key_of[0], (NB, NA), 1.0, 6.0, ((0, 256),), jnp.float32)
    alpha_table = bell_draw(key_of[1], (TYPES, BLOCK * BLOCK), (BLOCK * ALPHA_K) ** -0.5, 0.1875, (), jnp.float32)
    alpha_blocks = different_ones(key_of[2], NAB, NAB, ALPHA_K, 0)
    alpha_types = place_ends(jax.random.randint(key_of[3], (NAB, ALPHA_K), 0, TYPES), jax.random.fold_in(key_of[3], 1), 0, TYPES - 1).astype(jnp.int32)
    beta_table = bell_draw(key_of[4], (TYPES, BLOCK * BLOCK), (BLOCK * BETA_K) ** -0.5, 0.21875, (), jnp.float32)
    beta_blocks = different_ones(key_of[5], NBB, 2 * NBC, BETA_K, 0)
    beta_types = place_ends(jax.random.randint(key_of[6], (NBB, BETA_K), 0, TYPES), jax.random.fold_in(key_of[6], 1), 0, TYPES - 1).astype(jnp.int32)
    row_counts = ragged_sizes(key_of[7], N_COL, NA, CAP, 1).astype(jnp.int32)
    return dict(coeffs_t=coeffs_t, alpha_table=alpha_table, alpha_blocks=alpha_blocks, alpha_types=alpha_types, beta_table=beta_table, beta_blocks=beta_blocks, beta_types=beta_types, row_counts=row_counts)


exact_mode = lax.Precision.HIGHEST


def alpha_product(coeffs, alpha_table, alpha_blocks, alpha_types):
    blocked = coeffs.reshape(NA // BLOCK, BLOCK, NB)
    tables = alpha_table.reshape(TYPES, BLOCK, BLOCK)

    def one_block(block_id):
        source = jnp.take(blocked, alpha_blocks[block_id], axis=0)
        matrices = jnp.take(tables, alpha_types[block_id], axis=0)
        return jnp.einsum("kab,kbn->an", matrices, source, precision=exact_mode)

    results = lax.map(one_block, jnp.arange(NA // BLOCK, dtype=jnp.int32))
    return results.reshape(NA, NB)


def beta_product(coeffs, beta_table, beta_blocks, beta_types):
    per_class = NB // (BLOCK * N_CLS)
    blocked = coeffs.reshape(NA, NB // BLOCK, BLOCK)
    tables = beta_table.reshape(TYPES, BLOCK, BLOCK)

    def one_block(block_id):
        own_class = (block_id // per_class).astype(jnp.int32)
        other_class = jnp.bitwise_xor(own_class, 1).astype(jnp.int32)
        entries = beta_blocks[block_id]
        class_of = jnp.where(entries < per_class, own_class, other_class)
        global_id = (class_of * per_class + entries % per_class).astype(jnp.int32)
        source = jnp.take(blocked, global_id, axis=1)
        matrices = jnp.take(tables, beta_types[block_id], axis=0)
        return jnp.einsum("rka,kab->rb", source, matrices, precision=exact_mode)

    results = lax.map(one_block, jnp.arange(NB // BLOCK, dtype=jnp.int32))
    return jnp.transpose(results, (1, 0, 2)).reshape(NA, NB)


def reference(coeffs_t, alpha_table, alpha_blocks, alpha_types, beta_table, beta_blocks, beta_types, row_counts):
    coeffs = jnp.transpose(coeffs_t)
    sigma_total = alpha_product(coeffs, alpha_table, alpha_blocks, alpha_types)
    sigma_total = sigma_total + beta_product(coeffs, beta_table, beta_blocks, beta_types)
    starts = (jnp.cumsum(row_counts) - row_counts).astype(jnp.int32)
    offsets = jnp.arange(CAP, dtype=jnp.int32)
    row_index = (starts[:, None] + offsets[None, :]).reshape(-1).astype(jnp.int32)
    padded = jnp.concatenate([sigma_total, jnp.zeros((CAP, NB), jnp.float32)], 0)
    slot_rows = jnp.take(padded, row_index, axis=0)
    in_range = (offsets[None, :] < row_counts[:, None]).reshape(-1)
    return jnp.where(in_range[:, None], slot_rows, jnp.float32(0.0))
```

```python
import jax
import jax.numpy as jnp
from jax import lax
from jax.experimental import pallas as pl
from jax.experimental.pallas import tpu as pltpu
from jax.sharding import PartitionSpec as P

f32 = jnp.float32
bf16 = jnp.bfloat16

NA = 1024
BLK = 64
COLS = 32
CAP = 48
LOCAL = 192
HALF = CAP // 2
PACK = CAP + HALF
ROWS = NA + CAP + 8


def split(x):
    hi = x.astype(bf16)
    return hi, (x - hi.astype(f32)).astype(bf16)


def left_half(shape):
    return lax.broadcasted_iota(jnp.int32, shape, len(shape) - 1) < BLK


def load_transposed(x_ref, buf_ref):
    for c in range(NA // 128):
        cols = slice(128 * c, 128 * c + 128)
        last = x_ref[128:192, cols]
        buf_ref[cols, 0:128] = x_ref[0:128, cols].T
        buf_ref[cols, 128:256] = jnp.concatenate([last, last], 0).T


def write_slots(counts_ref, buf_ref, out_ref):
    buf_ref[NA:ROWS, :] = jnp.zeros((ROWS - NA, 256), f32)
    row = lax.broadcasted_iota(jnp.int32, (CAP, 128), 0)
    row_low = lax.broadcasted_iota(jnp.int32, (HALF, 128), 0)
    row_low = jnp.where(left_half((HALF, 128)), row_low, row_low + HALF)
    left = left_half((8, 128))
    sub = lax.broadcasted_iota(jnp.int32, (8, 256), 0)

    def one(j, start):
        count = counts_ref[j]
        base = pl.multiple_of((start // 8) * 8, 8)
        shift = 8 - (start - base)
        turned = [pltpu.roll(buf_ref[pl.ds(base + 8 * n, 8), :], shift & 7, 0) for n in range(CAP // 8 + 1)]
        rows = [jnp.where(sub < shift, turned[n], turned[n + 1]) for n in range(CAP // 8)]
        main = jnp.concatenate([r[:, 0:128] for r in rows], 0)
        out_ref[j, 0:CAP, :] = jnp.where(row < count, main, 0.0)
        third = [r[:, 128:256] for r in rows]
        folded = jnp.concatenate(
            [jnp.where(left, third[n], third[n + HALF // 8]) for n in range(HALF // 8)], 0
        )
        out_ref[j, CAP:PACK, :] = jnp.where(row_low < count, folded, 0.0)
        return start + count

    lax.fori_loop(0, COLS, one, jnp.int32(0))


def coeff_kernel(counts_ref, x_ref, out_ref, buf_ref):
    load_transposed(x_ref, buf_ref)
    write_slots(counts_ref, buf_ref, out_ref)


def alpha_kernel(counts_ref, blocks_ref, types_ref, x_ref, table_ref, out_ref, buf_ref, a_ref, hi_ref, lo_ref):
    load_transposed(x_ref, buf_ref)
    blocks = NA // BLK
    for b in range(blocks):
        hi, lo = split(buf_ref[BLK * b:BLK * b + BLK, :])
        for half in range(2):
            at = slice(128 * b + BLK * half, 128 * b + BLK * half + BLK)
            hi_ref[at, :] = hi
            lo_ref[at, :] = lo

    def place(i, carry):
        for k in range(blocks):
            col = pl.multiple_of(blocks_ref[i, k] * 128, 128)
            row = pl.multiple_of(i * BLK, BLK)
            a_ref[pl.ds(row, BLK), pl.ds(col, 128)] = table_ref[types_ref[i, k]]
        return carry

    lax.fori_loop(0, blocks, place, 0)
    for r in range(4):
        rows = slice(256 * r, 256 * r + 256)
        a = a_ref[rows, :]
        buf_ref[rows, :] = jnp.dot(a, hi_ref[...], preferred_element_type=f32) + jnp.dot(
            a, lo_ref[...], preferred_element_type=f32
        )
    write_slots(counts_ref, buf_ref, out_ref)


def beta_kernel(blocks_ref, types_ref, own_ref, partner_ref, alpha_ref, table_ref, out_ref, hi_ref, lo_ref):
    left = left_half((CAP, 128))
    left_low = left_half((HALF, 128))

    def swap(x):
        return pltpu.roll(x, BLK, 1)

    def unpack(ref, base):
        def one(j, carry):
            main = ref[j, 0:CAP, :]
            low = ref[j, CAP:PACK, :]
            main_r = swap(main)
            low_r = swap(low)
            parts = (
                jnp.where(left, main, main_r),
                jnp.where(left, main_r, main),
                jnp.concatenate([jnp.where(left_low, low, low_r), jnp.where(left_low, low_r, low)], 0),
            )
            for n in range(3):
                hi, lo = split(parts[n])
                hi_ref[base + 3 * j + n] = hi
                lo_ref[base + 3 * j + n] = lo
            return carry

        lax.fori_loop(0, COLS, one, 0)

    unpack(own_ref, 0)
    unpack(partner_ref, 96)

    def block(m):
        total = jnp.zeros((2 * CAP, 128), f32)
        for g in range(3):
            hi_parts, lo_parts, w_parts = [], [], []
            for q in range(2):
                s0 = blocks_ref[4 * g + 2 * q, m]
                s1 = blocks_ref[4 * g + 2 * q + 1, m]
                hi_parts.append(jnp.where(left, hi_ref[s0], hi_ref[s1]))
                lo_parts.append(jnp.where(left, lo_ref[s0], lo_ref[s1]))
                w_parts.append(table_ref[types_ref[4 * g + 2 * q, m]])
                w_parts.append(table_ref[types_ref[4 * g + 2 * q + 1, m]])
            lhs = jnp.concatenate([jnp.concatenate(hi_parts, 1), jnp.concatenate(lo_parts, 1)], 0)
            total = total + jnp.dot(lhs, jnp.concatenate(w_parts, 0), preferred_element_type=f32)
        both = total[0:CAP] + total[CAP:]
        return both + swap(both)

    def triple(u, carry):
        a_main, a_low = alpha_ref[2 * u, 0:CAP, :], alpha_ref[2 * u, CAP:PACK, :]
        b_main, b_low = alpha_ref[2 * u + 1, 0:CAP, :], alpha_ref[2 * u + 1, CAP:PACK, :]
        b_main_r = swap(b_main)
        alphas = (
            a_main,
            jnp.where(left, jnp.concatenate([a_low, swap(a_low)], 0), b_main_r),
            jnp.where(left, b_main_r, jnp.concatenate([swap(b_low), b_low], 0)),
        )
        for q in range(3):
            pair = jnp.where(left, block(6 * u + 2 * q), block(6 * u + 2 * q + 1))
            col = pl.multiple_of(u * 384 + 128 * q, 128)
            out_ref[:, pl.ds(col, 128)] = alphas[q] + pair
        return carry

    lax.fori_loop(0, COLS // 2, triple, 0)


def smem():
    return pl.BlockSpec(memory_space=pltpu.SMEM)


def vmem():
    return pl.BlockSpec(memory_space=pltpu.VMEM)


def split_table(table):
    tiles = table.reshape(table.shape[0], BLK, BLK)
    hi = lax.reduce_precision(tiles, 8, 7)
    return jnp.concatenate([hi, tiles - hi], 2).astype(bf16)


def on_device(coeffs_t, alpha_table, alpha_blocks, alpha_types, beta_table, beta_blocks, beta_types, row_counts):
    slots = jax.ShapeDtypeStruct((COLS, PACK, 128), f32)
    coeff_slots = pl.pallas_call(
        coeff_kernel,
        in_specs=[smem(), vmem()],
        out_specs=vmem(),
        out_shape=slots,
        scratch_shapes=[pltpu.VMEM((ROWS, 256), f32)],
        name="coeff_slots",
    )(row_counts, coeffs_t)
    alpha_slots = pl.pallas_call(
        alpha_kernel,
        in_specs=[smem(), smem(), smem(), vmem(), vmem()],
        out_specs=vmem(),
        out_shape=slots,
        scratch_shapes=[
            pltpu.VMEM((ROWS, 256), f32),
            pltpu.VMEM((NA, 2 * NA), bf16),
            pltpu.VMEM((2 * NA, 256), bf16),
            pltpu.VMEM((2 * NA, 256), bf16),
        ],
        name="alpha_slots",
    )(row_counts, alpha_blocks, alpha_types, coeffs_t, split_table(alpha_table))
    own = lax.all_to_all(coeff_slots, "col", split_axis=0, concat_axis=0, tiled=True)
    partner = lax.ppermute(own, "cls", [(i, i ^ 1) for i in range(8)])
    alpha = lax.all_to_all(alpha_slots, "col", split_axis=0, concat_axis=0, tiled=True)
    return pl.pallas_call(
        beta_kernel,
        in_specs=[smem(), smem(), vmem(), vmem(), vmem(), vmem()],
        out_specs=vmem(),
        out_shape=jax.ShapeDtypeStruct((CAP, 96 * BLK), f32),
        scratch_shapes=[pltpu.VMEM((192, CAP, 128), bf16), pltpu.VMEM((192, CAP, 128), bf16)],
        name="beta_sum",
    )(beta_blocks.T, beta_types.T, own, partner, alpha, split_table(beta_table))


def solution(mesh):
    return jax.shard_map(
        on_device,
        mesh=mesh,
        in_specs=(P(("cls", "col"), None), P(), P(), P(), P(), P("cls", None), P("cls", None), P()),
        out_specs=P("col", "cls"),
        check_vma=False,
    )
```

```python
import jax
import jax.numpy as jnp
from jax import lax
from jax.experimental import pallas as pl
from jax.experimental.pallas import tpu as pltpu
from jax.sharding import PartitionSpec as P

f32 = jnp.float32
bf16 = jnp.bfloat16

NA = 1024
BLK = 64
COLS = 32
CAP = 48
LOCAL = 192
HALF = CAP // 2
PACK = CAP + HALF
ROWS = NA + CAP + 8


def split(x):
    hi = x.astype(bf16)
    return hi, (x - hi.astype(f32)).astype(bf16)


def left_half(shape):
    return lax.broadcasted_iota(jnp.int32, shape, len(shape) - 1) < BLK


def load_transposed(x_ref, buf_ref):
    for c in range(NA // 128):
        cols = slice(128 * c, 128 * c + 128)
        last = x_ref[128:192, cols]
        buf_ref[cols, 0:128] = x_ref[0:128, cols].T
        buf_ref[cols, 128:256] = jnp.concatenate([last, last], 0).T


def write_slots(counts_ref, buf_ref, out_ref):
    buf_ref[NA:ROWS, :] = jnp.zeros((ROWS - NA, 256), f32)
    row = lax.broadcasted_iota(jnp.int32, (CAP, 128), 0)
    row_low = lax.broadcasted_iota(jnp.int32, (HALF, 128), 0)
    row_low = jnp.where(left_half((HALF, 128)), row_low, row_low + HALF)
    left = left_half((8, 128))
    sub = lax.broadcasted_iota(jnp.int32, (8, 256), 0)

    def one(j, start):
        count = counts_ref[j]
        base = pl.multiple_of((start // 8) * 8, 8)
        shift = 8 - (start - base)
        turned = [pltpu.roll(buf_ref[pl.ds(base + 8 * n, 8), :], shift & 7, 0) for n in range(CAP // 8 + 1)]
        rows = [jnp.where(sub < shift, turned[n], turned[n + 1]) for n in range(CAP // 8)]
        main = jnp.concatenate([r[:, 0:128] for r in rows], 0)
        out_ref[j, 0:CAP, :] = jnp.where(row < count, main, 0.0)
        third = [r[:, 128:256] for r in rows]
        folded = jnp.concatenate(
            [jnp.where(left, third[n], third[n + HALF // 8]) for n in range(HALF // 8)], 0
        )
        out_ref[j, CAP:PACK, :] = jnp.where(row_low < count, folded, 0.0)
        return start + count

    lax.fori_loop(0, COLS, one, jnp.int32(0))


def coeff_kernel(counts_ref, x_ref, out_ref, buf_ref):
    load_transposed(x_ref, buf_ref)
    write_slots(counts_ref, buf_ref, out_ref)


def alpha_kernel(counts_ref, blocks_ref, types_ref, x_ref, table_ref, out_ref, buf_ref, a_ref, hi_ref, lo_ref):
    load_transposed(x_ref, buf_ref)
    blocks = NA // BLK
    for b in range(blocks):
        hi, lo = split(buf_ref[BLK * b:BLK * b + BLK, :])
        for half in range(2):
            at = slice(128 * b + BLK * half, 128 * b + BLK * half + BLK)
            hi_ref[at, :] = hi
            lo_ref[at, :] = lo

    def place(i, carry):
        for k in range(blocks):
            col = pl.multiple_of(blocks_ref[i, k] * 128, 128)
            row = pl.multiple_of(i * BLK, BLK)
            a_ref[pl.ds(row, BLK), pl.ds(col, 128)] = table_ref[types_ref[i, k]]
        return carry

    lax.fori_loop(0, blocks, place, 0)
    for r in range(4):
        rows = slice(256 * r, 256 * r + 256)
        a = a_ref[rows, :]
        buf_ref[rows, :] = jnp.dot(a, hi_ref[...], preferred_element_type=f32) + jnp.dot(
            a, lo_ref[...], preferred_element_type=f32
        )
    write_slots(counts_ref, buf_ref, out_ref)


def swap(x):
    return pltpu.roll(x, BLK, 1)


def unpack(ref, x_ref, base):
    left = left_half((CAP, 128))
    left_low = left_half((HALF, 128))

    def one(j, carry):
        main = ref[j, 0:CAP, :]
        low = ref[j, CAP:PACK, :]
        main_r = swap(main)
        low_r = swap(low)
        main_lo = main - main.astype(bf16).astype(f32)
        low_lo = low - low.astype(bf16).astype(f32)
        main_lo_r = swap(main_lo)
        low_lo_r = swap(low_lo)
        x_ref[base + 3 * j] = jnp.where(left, main, main_lo_r).astype(bf16)
        x_ref[base + 3 * j + 1] = jnp.where(left, main_r, main_lo).astype(bf16)
        x_ref[base + 3 * j + 2] = jnp.concatenate(
            [jnp.where(left_low, low, low_lo_r), jnp.where(left_low, low_r, low_lo)], 0
        ).astype(bf16)
        return carry

    lax.fori_loop(0, COLS, one, 0)


def own_kernel(own_ref, x_ref):
    unpack(own_ref, x_ref, 0)


def beta_kernel(
    blocks_ref, types_ref, own_hbm, partner_hbm, alpha_hbm, table_hbm, out_hbm,
    x_ref, partner_ref, alpha_ref, table_ref, out_ref, sems, out_sems,
):
    own_copy = pltpu.make_async_copy(own_hbm, x_ref.at[0:96], sems.at[0])
    partner_copy = pltpu.make_async_copy(partner_hbm, partner_ref, sems.at[1])
    alpha_copy = pltpu.make_async_copy(alpha_hbm, alpha_ref, sems.at[2])
    table_copy = pltpu.make_async_copy(table_hbm, table_ref, sems.at[3])
    partner_copy.start()
    own_copy.start()
    table_copy.start()
    alpha_copy.start()
    left = left_half((CAP, 128))
    partner_copy.wait()
    unpack(partner_ref, x_ref, 96)
    own_copy.wait()
    table_copy.wait()
    alpha_copy.wait()

    def block(m):
        lhs, rhs = [], []
        for k in range(12):
            lhs.append(x_ref[blocks_ref[k, m]])
            w = table_ref[types_ref[k, m]]
            rhs += [w, w]
        both = jnp.dot(jnp.concatenate(lhs, 1), jnp.concatenate(rhs, 0), preferred_element_type=f32)
        return both + swap(both)

    def triple(u, carry):
        a_main, a_low = alpha_ref[2 * u, 0:CAP, :], alpha_ref[2 * u, CAP:PACK, :]
        b_main, b_low = alpha_ref[2 * u + 1, 0:CAP, :], alpha_ref[2 * u + 1, CAP:PACK, :]
        b_main_r = swap(b_main)
        alphas = (
            a_main,
            jnp.where(left, jnp.concatenate([a_low, swap(a_low)], 0), b_main_r),
            jnp.where(left, b_main_r, jnp.concatenate([swap(b_low), b_low], 0)),
        )
        for q in range(3):
            pair = jnp.where(left, block(6 * u + 2 * q), block(6 * u + 2 * q + 1))
            col = pl.multiple_of(u * 384 + 128 * q, 128)
            out_ref[:, pl.ds(col, 128)] = alphas[q] + pair
        return carry

    copies = []
    for part in range(4):
        lax.fori_loop(4 * part, 4 * part + 4, triple, 0)
        cols = slice(1536 * part, 1536 * part + 1536)
        copy = pltpu.make_async_copy(out_ref.at[:, cols], out_hbm.at[:, cols], out_sems.at[part])
        copy.start()
        copies.append(copy)
    for copy in copies:
        copy.wait()


def smem():
    return pl.BlockSpec(memory_space=pltpu.SMEM)


def vmem():
    return pl.BlockSpec(memory_space=pltpu.VMEM)


def hbm():
    return pl.BlockSpec(memory_space=pl.ANY)


def split_table(table):
    tiles = table.reshape(table.shape[0], BLK, BLK)
    hi = lax.reduce_precision(tiles, 8, 7)
    return jnp.concatenate([hi, tiles - hi], 2).astype(bf16)


def on_device(coeffs_t, alpha_table, alpha_blocks, alpha_types, beta_table, beta_blocks, beta_types, row_counts):
    slots = jax.ShapeDtypeStruct((COLS, PACK, 128), f32)
    coeff_slots = pl.pallas_call(
        coeff_kernel,
        in_specs=[smem(), vmem()],
        out_specs=vmem(),
        out_shape=slots,
        scratch_shapes=[pltpu.VMEM((ROWS, 256), f32)],
        name="coeff_slots",
    )(row_counts, coeffs_t)
    alpha_slots = pl.pallas_call(
        alpha_kernel,
        in_specs=[smem(), smem(), smem(), vmem(), vmem()],
        out_specs=vmem(),
        out_shape=slots,
        scratch_shapes=[
            pltpu.VMEM((ROWS, 256), f32),
            pltpu.VMEM((NA, 2 * NA), bf16),
            pltpu.VMEM((2 * NA, 256), bf16),
            pltpu.VMEM((2 * NA, 256), bf16),
        ],
        name="alpha_slots",
    )(row_counts, alpha_blocks, alpha_types, coeffs_t, split_table(alpha_table))
    own = lax.all_to_all(coeff_slots, "col", split_axis=0, concat_axis=0, tiled=True)
    own, alpha_slots = lax.optimization_barrier((own, alpha_slots))
    partner = lax.ppermute(own, "cls", [(i, i ^ 1) for i in range(8)])
    alpha = lax.all_to_all(alpha_slots, "col", split_axis=0, concat_axis=0, tiled=True)
    own_x = pl.pallas_call(
        own_kernel,
        in_specs=[vmem()],
        out_specs=vmem(),
        out_shape=jax.ShapeDtypeStruct((96, CAP, 128), bf16),
        name="own_split",
    )(own)
    return pl.pallas_call(
        beta_kernel,
        in_specs=[smem(), smem(), hbm(), hbm(), hbm(), hbm()],
        out_specs=hbm(),
        out_shape=jax.ShapeDtypeStruct((CAP, 96 * BLK), f32),
        scratch_shapes=[
            pltpu.VMEM((192, CAP, 128), bf16),
            pltpu.VMEM((COLS, PACK, 128), f32),
            pltpu.VMEM((COLS, PACK, 128), f32),
            pltpu.VMEM((64, BLK, 128), bf16),
            pltpu.VMEM((CAP, 96 * BLK), f32),
            pltpu.SemaphoreType.DMA((4,)),
            pltpu.SemaphoreType.DMA((4,)),
        ],
        name="beta_sum",
    )(beta_blocks.T, beta_types.T, own_x, partner, alpha, split_table(beta_table))


def solution(mesh):
    return jax.shard_map(
        on_device,
        mesh=mesh,
        in_specs=(P(("cls", "col"), None), P(), P(), P(), P(), P("cls", None), P("cls", None), P()),
        out_specs=P("col", "cls"),
        check_vma=False,
    )
```

```python
import jax
import jax.numpy as jnp
from jax import lax
from jax.experimental import pallas as pl
from jax.experimental.pallas import tpu as pltpu
from jax.sharding import PartitionSpec as P

f32 = jnp.float32
bf16 = jnp.bfloat16

NA = 1024
BLK = 64
COLS = 32
CAP = 48
LOCAL = 192
HALF = CAP // 2
PACK = CAP + HALF
ROWS = NA + CAP + 8


def split(x):
    hi = x.astype(bf16)
    return hi, (x - hi.astype(f32)).astype(bf16)


def left_half(shape):
    return lax.broadcasted_iota(jnp.int32, shape, len(shape) - 1) < BLK


def load_transposed(x_ref, buf_ref):
    for c in range(NA // 128):
        cols = slice(128 * c, 128 * c + 128)
        last = x_ref[128:192, cols]
        buf_ref[cols, 0:128] = x_ref[0:128, cols].T
        buf_ref[cols, 128:256] = jnp.concatenate([last, last], 0).T


def write_slots(counts_ref, buf_ref, out_ref):
    buf_ref[NA:ROWS, :] = jnp.zeros((ROWS - NA, 256), f32)
    row = lax.broadcasted_iota(jnp.int32, (CAP, 128), 0)
    row_low = lax.broadcasted_iota(jnp.int32, (HALF, 128), 0)
    row_low = jnp.where(left_half((HALF, 128)), row_low, row_low + HALF)
    left = left_half((8, 128))
    sub = lax.broadcasted_iota(jnp.int32, (8, 256), 0)

    def one(j, start):
        count = counts_ref[j]
        base = pl.multiple_of((start // 8) * 8, 8)
        shift = 8 - (start - base)
        turned = [pltpu.roll(buf_ref[pl.ds(base + 8 * n, 8), :], shift & 7, 0) for n in range(CAP // 8 + 1)]
        rows = [jnp.where(sub < shift, turned[n], turned[n + 1]) for n in range(CAP // 8)]
        main = jnp.concatenate([r[:, 0:128] for r in rows], 0)
        out_ref[j, 0:CAP, :] = jnp.where(row < count, main, 0.0)
        third = [r[:, 128:256] for r in rows]
        folded = jnp.concatenate(
            [jnp.where(left, third[n], third[n + HALF // 8]) for n in range(HALF // 8)], 0
        )
        out_ref[j, CAP:PACK, :] = jnp.where(row_low < count, folded, 0.0)
        return start + count

    lax.fori_loop(0, COLS, one, jnp.int32(0))


def coeff_kernel(counts_ref, x_ref, out_ref, buf_ref):
    load_transposed(x_ref, buf_ref)
    write_slots(counts_ref, buf_ref, out_ref)


def alpha_kernel(counts_ref, blocks_ref, types_ref, x_ref, table_ref, out_ref, buf_ref, a_ref, hi_ref, lo_ref):
    load_transposed(x_ref, buf_ref)
    blocks = NA // BLK
    for b in range(blocks):
        hi, lo = split(buf_ref[BLK * b:BLK * b + BLK, :])
        for half in range(2):
            at = slice(128 * b + BLK * half, 128 * b + BLK * half + BLK)
            hi_ref[at, :] = hi
            lo_ref[at, :] = lo

    def place(i, carry):
        for k in range(blocks):
            col = pl.multiple_of(blocks_ref[i, k] * 128, 128)
            row = pl.multiple_of(i * BLK, BLK)
            a_ref[pl.ds(row, BLK), pl.ds(col, 128)] = table_ref[types_ref[i, k]]
        return carry

    lax.fori_loop(0, blocks, place, 0)
    for r in range(4):
        rows = slice(256 * r, 256 * r + 256)
        a = a_ref[rows, :]
        buf_ref[rows, :] = jnp.dot(a, hi_ref[...], preferred_element_type=f32) + jnp.dot(
            a, lo_ref[...], preferred_element_type=f32
        )
    write_slots(counts_ref, buf_ref, out_ref)


def swap(x):
    return pltpu.roll(x, BLK, 1)


def unpack(ref, z_ref, base):
    left = left_half((CAP, 128))
    left_low = left_half((HALF, 128))

    def one(j, carry):
        main = ref[j, 0:CAP, :]
        low = ref[j, CAP:PACK, :]
        main_r = swap(main)
        low_r = swap(low)
        parts = (
            jnp.where(left, main, main_r),
            jnp.where(left, main_r, main),
            jnp.concatenate([jnp.where(left_low, low, low_r), jnp.where(left_low, low_r, low)], 0),
        )
        for n in range(3):
            hi, lo = split(parts[n])
            z_ref[base + 3 * j + n] = jnp.concatenate([hi, lo], 1)
        return carry

    lax.fori_loop(0, COLS, one, 0)


def own_kernel(own_ref, x_ref):
    unpack(own_ref, x_ref, 0)


def beta_kernel(
    blocks_ref, types_ref, own_hbm, partner_hbm, alpha_hbm, table_hbm, out_hbm,
    x_ref, partner_ref, alpha_ref, table_ref, out_ref, sems, out_sems,
):
    own_copy = pltpu.make_async_copy(own_hbm, x_ref.at[0:96], sems.at[0])
    partner_copy = pltpu.make_async_copy(partner_hbm, partner_ref, sems.at[1])
    alpha_copy = pltpu.make_async_copy(alpha_hbm, alpha_ref, sems.at[2])
    table_copy = pltpu.make_async_copy(table_hbm, table_ref, sems.at[3])
    partner_copy.start()
    own_copy.start()
    table_copy.start()
    alpha_copy.start()
    left = left_half((CAP, 128))
    partner_copy.wait()
    unpack(partner_ref, x_ref, 96)
    own_copy.wait()
    table_copy.wait()
    alpha_copy.wait()

    pick = left_half((CAP, 256)) | (lax.broadcasted_iota(jnp.int32, (CAP, 256), 1) // BLK == 2)

    def block(m):
        hi, lo, w = [], [], []
        for k in range(0, 12, 2):
            pair = jnp.where(pick, x_ref[blocks_ref[k, m]], x_ref[blocks_ref[k + 1, m]])
            hi.append(pair[:, 0:128])
            lo.append(pair[:, 128:256])
            w.append(table_ref[types_ref[k, m]])
            w.append(table_ref[types_ref[k + 1, m]])
        lhs = jnp.concatenate([jnp.concatenate(hi, 1), jnp.concatenate(lo, 1)], 0)
        both = jnp.dot(lhs, jnp.concatenate(w, 0), preferred_element_type=f32)
        both = both[0:CAP] + both[CAP:]
        return both + swap(both)

    def triples(n, carry):
        for half in range(2):
            triple(2 * n + half)
        return carry

    def triple(u):
        a_main, a_low = alpha_ref[2 * u, 0:CAP, :], alpha_ref[2 * u, CAP:PACK, :]
        b_main, b_low = alpha_ref[2 * u + 1, 0:CAP, :], alpha_ref[2 * u + 1, CAP:PACK, :]
        b_main_r = swap(b_main)
        alphas = (
            a_main,
            jnp.where(left, jnp.concatenate([a_low, swap(a_low)], 0), b_main_r),
            jnp.where(left, b_main_r, jnp.concatenate([swap(b_low), b_low], 0)),
        )
        for q in range(3):
            pair = jnp.where(left, block(6 * u + 2 * q), block(6 * u + 2 * q + 1))
            col = pl.multiple_of(u * 384 + 128 * q, 128)
            out_ref[:, pl.ds(col, 128)] = alphas[q] + pair

    copies = []
    for part in range(4):
        lax.fori_loop(2 * part, 2 * part + 2, triples, 0)
        cols = slice(1536 * part, 1536 * part + 1536)
        copy = pltpu.make_async_copy(out_ref.at[:, cols], out_hbm.at[:, cols], out_sems.at[part])
        copy.start()
        copies.append(copy)
    for copy in copies:
        copy.wait()


def smem():
    return pl.BlockSpec(memory_space=pltpu.SMEM)


def vmem():
    return pl.BlockSpec(memory_space=pltpu.VMEM)


def hbm():
    return pl.BlockSpec(memory_space=pl.ANY)


def split_table(table):
    tiles = table.reshape(table.shape[0], BLK, BLK)
    hi = lax.reduce_precision(tiles, 8, 7)
    return jnp.concatenate([hi, tiles - hi], 2).astype(bf16)


def on_device(coeffs_t, alpha_table, alpha_blocks, alpha_types, beta_table, beta_blocks, beta_types, row_counts):
    slots = jax.ShapeDtypeStruct((COLS, PACK, 128), f32)
    coeff_slots = pl.pallas_call(
        coeff_kernel,
        in_specs=[smem(), vmem()],
        out_specs=vmem(),
        out_shape=slots,
        scratch_shapes=[pltpu.VMEM((ROWS, 256), f32)],
        name="coeff_slots",
    )(row_counts, coeffs_t)
    alpha_slots = pl.pallas_call(
        alpha_kernel,
        in_specs=[smem(), smem(), smem(), vmem(), vmem()],
        out_specs=vmem(),
        out_shape=slots,
        scratch_shapes=[
            pltpu.VMEM((ROWS, 256), f32),
            pltpu.VMEM((NA, 2 * NA), bf16),
            pltpu.VMEM((2 * NA, 256), bf16),
            pltpu.VMEM((2 * NA, 256), bf16),
        ],
        name="alpha_slots",
    )(row_counts, alpha_blocks, alpha_types, coeffs_t, split_table(alpha_table))
    own = lax.all_to_all(coeff_slots, "col", split_axis=0, concat_axis=0, tiled=True)
    own, alpha_slots = lax.optimization_barrier((own, alpha_slots))
    partner = lax.ppermute(own, "cls", [(i, i ^ 1) for i in range(8)])
    alpha = lax.all_to_all(alpha_slots, "col", split_axis=0, concat_axis=0, tiled=True)
    own_x = pl.pallas_call(
        own_kernel,
        in_specs=[vmem()],
        out_specs=vmem(),
        out_shape=jax.ShapeDtypeStruct((96, CAP, 256), bf16),
        name="own_split",
    )(own)
    return pl.pallas_call(
        beta_kernel,
        in_specs=[smem(), smem(), hbm(), hbm(), hbm(), hbm()],
        out_specs=hbm(),
        out_shape=jax.ShapeDtypeStruct((CAP, 96 * BLK), f32),
        scratch_shapes=[
            pltpu.VMEM((192, CAP, 256), bf16),
            pltpu.VMEM((COLS, PACK, 128), f32),
            pltpu.VMEM((COLS, PACK, 128), f32),
            pltpu.VMEM((64, BLK, 128), bf16),
            pltpu.VMEM((CAP, 96 * BLK), f32),
            pltpu.SemaphoreType.DMA((4,)),
            pltpu.SemaphoreType.DMA((4,)),
        ],
        name="beta_sum",
    )(beta_blocks.T, beta_types.T, own_x, partner, alpha, split_table(beta_table))


def solution(mesh):
    return jax.shard_map(
        on_device,
        mesh=mesh,
        in_specs=(P(("cls", "col"), None), P(), P(), P(), P(), P("cls", None), P("cls", None), P()),
        out_specs=P("col", "cls"),
        check_vma=False,
    )
```

```python
import jax
import jax.numpy as jnp
from jax import lax
from jax.experimental import pallas as pl
from jax.experimental.pallas import tpu as pltpu
from jax.sharding import PartitionSpec as P

f32 = jnp.float32
bf16 = jnp.bfloat16

NA = 1024
BLK = 64
COLS = 32
CAP = 48
HALF = CAP // 2
PACK = CAP + HALF
BLOCKS = 96
DEPTH = 12
FIRST = 22
BOUNDS = (0, BLOCKS, BLOCKS + 3 * FIRST, 2 * BLOCKS)
UNROLL = 32
LIST = 640
ROWS = NA + CAP + 8


def split(x):
    hi = x.astype(bf16)
    return hi, (x - hi.astype(f32)).astype(bf16)


def left_half(shape):
    return lax.broadcasted_iota(jnp.int32, shape, len(shape) - 1) < BLK


def load_transposed(x_ref, buf_ref):
    for c in range(NA // 128):
        cols = slice(128 * c, 128 * c + 128)
        last = x_ref[128:192, cols]
        buf_ref[cols, 0:128] = x_ref[0:128, cols].T
        buf_ref[cols, 128:256] = jnp.concatenate([last, last], 0).T


def write_slots(counts_ref, buf_ref, out_ref):
    buf_ref[NA:ROWS, :] = jnp.zeros((ROWS - NA, 256), f32)
    row = lax.broadcasted_iota(jnp.int32, (CAP, 128), 0)
    row_low = lax.broadcasted_iota(jnp.int32, (HALF, 128), 0)
    row_low = jnp.where(left_half((HALF, 128)), row_low, row_low + HALF)
    left = left_half((8, 128))
    sub = lax.broadcasted_iota(jnp.int32, (8, 256), 0)

    def one(j, start):
        count = counts_ref[j]
        base = pl.multiple_of((start // 8) * 8, 8)
        shift = 8 - (start - base)
        turned = [pltpu.roll(buf_ref[pl.ds(base + 8 * n, 8), :], shift & 7, 0) for n in range(CAP // 8 + 1)]
        rows = [jnp.where(sub < shift, turned[n], turned[n + 1]) for n in range(CAP // 8)]
        main = jnp.concatenate([r[:, 0:128] for r in rows], 0)
        out_ref[j, 0:CAP, :] = jnp.where(row < count, main, 0.0)
        third = [r[:, 128:256] for r in rows]
        folded = jnp.concatenate(
            [jnp.where(left, third[n], third[n + HALF // 8]) for n in range(HALF // 8)], 0
        )
        out_ref[j, CAP:PACK, :] = jnp.where(row_low < count, folded, 0.0)
        return start + count

    lax.fori_loop(0, COLS, one, jnp.int32(0))


def coeff_kernel(counts_ref, x_ref, out_ref, buf_ref):
    load_transposed(x_ref, buf_ref)
    write_slots(counts_ref, buf_ref, out_ref)


def alpha_kernel(counts_ref, blocks_ref, types_ref, x_ref, table_ref, out_ref, buf_ref, a_ref, hi_ref, lo_ref):
    load_transposed(x_ref, buf_ref)
    blocks = NA // BLK
    for b in range(blocks):
        hi, lo = split(buf_ref[BLK * b:BLK * b + BLK, :])
        for half in range(2):
            at = slice(128 * b + BLK * half, 128 * b + BLK * half + BLK)
            hi_ref[at, :] = hi
            lo_ref[at, :] = lo

    def place(i, carry):
        for k in range(blocks):
            col = pl.multiple_of(blocks_ref[i, k] * 128, 128)
            row = pl.multiple_of(i * BLK, BLK)
            a_ref[pl.ds(row, BLK), pl.ds(col, 128)] = table_ref[types_ref[i, k]]
        return carry

    lax.fori_loop(0, blocks, place, 0)
    for r in range(4):
        rows = slice(256 * r, 256 * r + 256)
        a = a_ref[rows, :]
        buf_ref[rows, :] = jnp.dot(a, hi_ref[...], preferred_element_type=f32) + jnp.dot(
            a, lo_ref[...], preferred_element_type=f32
        )
    write_slots(counts_ref, buf_ref, out_ref)


def swap(x):
    return pltpu.roll(x, BLK, 1)


def unpack(ref, senders, x_ref):
    left = left_half((CAP, 128))
    left_low = left_half((HALF, 128))

    def one(j, carry):
        main = ref[j, 0:CAP, :]
        low = ref[j, CAP:PACK, :]
        main_lo = main - main.astype(bf16).astype(f32)
        low_lo = low - low.astype(bf16).astype(f32)
        main_r, low_r, main_lo_r, low_lo_r = swap(main), swap(low), swap(main_lo), swap(low_lo)
        x_ref[3 * j] = jnp.where(left, main, main_lo_r).astype(bf16)
        x_ref[3 * j + 1] = jnp.where(left, main_r, main_lo).astype(bf16)
        x_ref[3 * j + 2] = jnp.concatenate(
            [jnp.where(left_low, low, low_lo_r), jnp.where(left_low, low_r, low_lo)], 0
        ).astype(bf16)
        return carry

    lax.fori_loop(0, senders, one, 0)
    x_ref[3 * senders] = jnp.zeros((CAP, 128), bf16)


def plan_kernel(blocks_ref, types_ref, words_ref, lists_ref, totals_ref, entry_ref, counts_ref, smem_ref, sem):
    entry_ref[...] = jnp.full((16, 128), 1 << 20, jnp.int32)
    entry_ref[0:DEPTH, 0:BLOCKS] = blocks_ref[...]
    entries = entry_ref[...]
    entry_ref[...] = jnp.zeros((16, 128), jnp.int32)
    entry_ref[0:DEPTH, 0:BLOCKS] = types_ref[...]
    types = entry_ref[...]
    row = lax.broadcasted_iota(jnp.int32, (16, 128), 0)
    counts_ref[...] = jnp.zeros((8, 128), jnp.int32)
    for q in range(3):
        low, high = BOUNDS[q], BOUNDS[q + 1]
        held = jnp.where((entries >= low) & (entries < high), 1, 0)
        word = (types << 8) | (entries - low)
        rank = jnp.zeros((1, 128), jnp.int32)
        ordered = jnp.full((16, 128), high - low, jnp.int32)
        for k in range(DEPTH):
            here = (row == rank) & (held[k:k + 1] > 0)
            ordered = jnp.where(here, word[k:k + 1], ordered)
            rank = rank + held[k:k + 1]
        words_ref[q] = ordered
        counts_ref[q:q + 1, :] = (rank + 1) >> 1
    copy = pltpu.make_async_copy(counts_ref, smem_ref, sem)
    copy.start()
    copy.wait()
    for q in range(3):

        def add(m, at):
            for i in range(DEPTH // 2):
                lists_ref[q, at + i] = m * 8 + i
            return at + smem_ref[q, m]

        end = lax.fori_loop(0, BLOCKS, add, jnp.int32(0))
        for i in range(UNROLL):
            lists_ref[q, end + i] = BLOCKS * 8
        totals_ref[q] = (end + UNROLL - 1) // UNROLL


def accumulate(q, words_ref, lists_ref, totals_ref, x_ref, table_ref, acc_ref):
    def batch(n, carry):
        for i in range(UNROLL):
            item = lists_ref[q, n * UNROLL + i]
            m = item >> 3
            pair = (item & 7) * 2
            w0 = words_ref[q, pair, m]
            w1 = words_ref[q, pair + 1, m]
            t0 = table_ref[w0 >> 8]
            t1 = table_ref[w1 >> 8]
            lhs = jnp.concatenate([x_ref[w0 & 255], x_ref[w1 & 255]], 1)
            rhs = jnp.concatenate([t0, t0, t1, t1], 0)
            acc_ref[m] = acc_ref[m] + jnp.dot(lhs, rhs, preferred_element_type=f32)
        return carry

    lax.fori_loop(0, totals_ref[q], batch, 0)


def zero(acc_ref):
    def one(m, carry):
        acc_ref[m] = jnp.zeros((CAP, 128), f32)
        return carry

    lax.fori_loop(0, BLOCKS + 1, one, 0)


def folded(acc_ref, pair, left):
    a = acc_ref[2 * pair]
    b = acc_ref[2 * pair + 1]
    return jnp.where(left, a + swap(a), b + swap(b))


def own_kernel(words_ref, lists_ref, totals_ref, own_ref, table_ref, acc_ref, x_ref):
    zero(acc_ref)
    unpack(own_ref, COLS, x_ref)
    accumulate(0, words_ref, lists_ref, totals_ref, x_ref, table_ref, acc_ref)


def first_kernel(words_ref, lists_ref, totals_ref, partner_ref, table_ref, prior_hbm, out_ref, x_ref, acc_ref, sem):
    copy = pltpu.make_async_copy(prior_hbm, acc_ref, sem)
    copy.start()
    unpack(partner_ref, FIRST, x_ref)
    copy.wait()
    accumulate(1, words_ref, lists_ref, totals_ref, x_ref, table_ref, acc_ref)
    left = left_half((CAP, 128))

    def one(p, carry):
        out_ref[:, pl.ds(pl.multiple_of(p * 128, 128), 128)] = folded(acc_ref, p, left)
        return carry

    lax.fori_loop(0, BLOCKS // 2, one, 0)


def last_kernel(
    words_ref, lists_ref, totals_ref, partner_ref, table_ref, prior_hbm, alpha_hbm, out_hbm,
    x_ref, acc_ref, prior_ref, alpha_ref, out_ref, sems, out_sems,
):
    prior_copy = pltpu.make_async_copy(prior_hbm, prior_ref, sems.at[0])
    alpha_copy = pltpu.make_async_copy(alpha_hbm, alpha_ref, sems.at[1])
    prior_copy.start()
    alpha_copy.start()
    zero(acc_ref)
    unpack(partner_ref, COLS - FIRST, x_ref)
    accumulate(2, words_ref, lists_ref, totals_ref, x_ref, table_ref, acc_ref)
    prior_copy.wait()
    alpha_copy.wait()
    left = left_half((CAP, 128))

    def triple(u, carry):
        a_main, a_low = alpha_ref[2 * u, 0:CAP, :], alpha_ref[2 * u, CAP:PACK, :]
        b_main, b_low = alpha_ref[2 * u + 1, 0:CAP, :], alpha_ref[2 * u + 1, CAP:PACK, :]
        b_main_r = swap(b_main)
        alphas = (
            a_main,
            jnp.where(left, jnp.concatenate([a_low, swap(a_low)], 0), b_main_r),
            jnp.where(left, b_main_r, jnp.concatenate([swap(b_low), b_low], 0)),
        )
        for n in range(3):
            col = pl.ds(pl.multiple_of(u * 384 + 128 * n, 128), 128)
            out_ref[:, col] = alphas[n] + (prior_ref[:, col] + folded(acc_ref, 3 * u + n, left))
        return carry

    copies = []
    for part in range(4):
        lax.fori_loop(4 * part, 4 * part + 4, triple, 0)
        cols = slice(1536 * part, 1536 * part + 1536)
        copy = pltpu.make_async_copy(out_ref.at[:, cols], out_hbm.at[:, cols], out_sems.at[part])
        copy.start()
        copies.append(copy)
    for copy in copies:
        copy.wait()


def smem():
    return pl.BlockSpec(memory_space=pltpu.SMEM)


def vmem():
    return pl.BlockSpec(memory_space=pltpu.VMEM)


def hbm():
    return pl.BlockSpec(memory_space=pl.ANY)


def split_table(table):
    tiles = table.reshape(table.shape[0], BLK, BLK)
    hi = lax.reduce_precision(tiles, 8, 7)
    return jnp.concatenate([hi, tiles - hi], 2).astype(bf16)


def on_device(coeffs_t, alpha_table, alpha_blocks, alpha_types, beta_table, beta_blocks, beta_types, row_counts):
    slots = jax.ShapeDtypeStruct((COLS, PACK, 128), f32)
    coeff_slots = pl.pallas_call(
        coeff_kernel,
        in_specs=[smem(), vmem()],
        out_specs=vmem(),
        out_shape=slots,
        scratch_shapes=[pltpu.VMEM((ROWS, 256), f32)],
        name="coeff_slots",
    )(row_counts, coeffs_t)
    alpha_slots = pl.pallas_call(
        alpha_kernel,
        in_specs=[smem(), smem(), smem(), vmem(), vmem()],
        out_specs=vmem(),
        out_shape=slots,
        scratch_shapes=[
            pltpu.VMEM((ROWS, 256), f32),
            pltpu.VMEM((NA, 2 * NA), bf16),
            pltpu.VMEM((2 * NA, 256), bf16),
            pltpu.VMEM((2 * NA, 256), bf16),
        ],
        name="alpha_slots",
    )(row_counts, alpha_blocks, alpha_types, coeffs_t, split_table(alpha_table))
    words, lists, totals = pl.pallas_call(
        plan_kernel,
        in_specs=[vmem(), vmem()],
        out_specs=[vmem(), smem(), smem()],
        out_shape=[
            jax.ShapeDtypeStruct((3, 16, 128), jnp.int32),
            jax.ShapeDtypeStruct((3, LIST), jnp.int32),
            jax.ShapeDtypeStruct((3,), jnp.int32),
        ],
        scratch_shapes=[
            pltpu.VMEM((16, 128), jnp.int32),
            pltpu.VMEM((8, 128), jnp.int32),
            pltpu.SMEM((8, 128), jnp.int32),
            pltpu.SemaphoreType.DMA,
        ],
        name="beta_plan",
    )(beta_blocks.T, beta_types.T)
    tiles = split_table(beta_table)
    own = lax.all_to_all(coeff_slots, "col", split_axis=0, concat_axis=0, tiled=True)
    own, alpha_slots, tiles, words, lists, totals = lax.optimization_barrier(
        (own, alpha_slots, tiles, words, lists, totals)
    )
    route = [(i, i ^ 1) for i in range(8)]
    partner_first = lax.ppermute(own[:FIRST], "cls", route)
    alpha = lax.all_to_all(alpha_slots, "col", split_axis=0, concat_axis=0, tiled=True)
    acc_shape = (BLOCKS + 1, CAP, 128)
    acc = pl.pallas_call(
        own_kernel,
        in_specs=[smem(), smem(), smem(), vmem(), vmem()],
        out_specs=vmem(),
        out_shape=jax.ShapeDtypeStruct(acc_shape, f32),
        scratch_shapes=[pltpu.VMEM((3 * COLS + 1, CAP, 128), bf16)],
        name="beta_own",
    )(words, lists, totals, own, tiles)
    rest, acc = lax.optimization_barrier((own[FIRST:], acc))
    partner_last = lax.ppermute(rest, "cls", route)
    prior = pl.pallas_call(
        first_kernel,
        in_specs=[smem(), smem(), smem(), vmem(), vmem(), hbm()],
        out_specs=vmem(),
        out_shape=jax.ShapeDtypeStruct((CAP, BLOCKS * BLK), f32),
        scratch_shapes=[
            pltpu.VMEM((3 * FIRST + 1, CAP, 128), bf16),
            pltpu.VMEM(acc_shape, f32),
            pltpu.SemaphoreType.DMA,
        ],
        name="beta_first",
    )(words, lists, totals, partner_first, tiles, acc)
    return pl.pallas_call(
        last_kernel,
        in_specs=[smem(), smem(), smem(), vmem(), vmem(), hbm(), hbm()],
        out_specs=hbm(),
        out_shape=jax.ShapeDtypeStruct((CAP, BLOCKS * BLK), f32),
        scratch_shapes=[
            pltpu.VMEM((3 * (COLS - FIRST) + 1, CAP, 128), bf16),
            pltpu.VMEM(acc_shape, f32),
            pltpu.VMEM((CAP, BLOCKS * BLK), f32),
            pltpu.VMEM((COLS, PACK, 128), f32),
            pltpu.VMEM((CAP, BLOCKS * BLK), f32),
            pltpu.SemaphoreType.DMA((2,)),
            pltpu.SemaphoreType.DMA((4,)),
        ],
        name="beta_last",
    )(words, lists, totals, partner_last, tiles, prior, alpha)


def solution(mesh):
    return jax.shard_map(
        on_device,
        mesh=mesh,
        in_specs=(P(("cls", "col"), None), P(), P(), P(), P(), P("cls", None), P("cls", None), P()),
        out_specs=P("col", "cls"),
        check_vma=False,
    )
```

```python
import jax
import jax.numpy as jnp
from jax import lax
from jax.experimental import pallas as pl
from jax.experimental.pallas import tpu as pltpu
from jax.sharding import PartitionSpec as P

f32 = jnp.float32
bf16 = jnp.bfloat16

NA = 1024
BLK = 64
COLS = 32
CAP = 48
HALF = CAP // 2
PACK = CAP + HALF
BLOCKS = 96
DEPTH = 12
FIRST = 24
BOUNDS = (0, BLOCKS, BLOCKS + 3 * FIRST, 2 * BLOCKS)
UNROLL = 32
GROUP = 4
LIST = 384
ROWS = NA + CAP + 8


def split(x):
    hi = x.astype(bf16)
    return hi, (x - hi.astype(f32)).astype(bf16)


def left_half(shape):
    return lax.broadcasted_iota(jnp.int32, shape, len(shape) - 1) < BLK


def load_transposed(x_ref, buf_ref):
    for c in range(NA // 128):
        cols = slice(128 * c, 128 * c + 128)
        last = x_ref[128:192, cols]
        buf_ref[cols, 0:128] = x_ref[0:128, cols].T
        buf_ref[cols, 128:256] = jnp.concatenate([last, last], 0).T


def write_slots(counts_ref, buf_ref, out_ref):
    buf_ref[NA:ROWS, :] = jnp.zeros((ROWS - NA, 256), f32)
    row = lax.broadcasted_iota(jnp.int32, (CAP, 128), 0)
    row_low = lax.broadcasted_iota(jnp.int32, (HALF, 128), 0)
    row_low = jnp.where(left_half((HALF, 128)), row_low, row_low + HALF)
    left = left_half((8, 128))
    sub = lax.broadcasted_iota(jnp.int32, (8, 256), 0)

    def one(j, start):
        count = counts_ref[j]
        base = pl.multiple_of((start // 8) * 8, 8)
        shift = 8 - (start - base)
        turned = [pltpu.roll(buf_ref[pl.ds(base + 8 * n, 8), :], shift & 7, 0) for n in range(CAP // 8 + 1)]
        rows = [jnp.where(sub < shift, turned[n], turned[n + 1]) for n in range(CAP // 8)]
        main = jnp.concatenate([r[:, 0:128] for r in rows], 0)
        out_ref[j, 0:CAP, :] = jnp.where(row < count, main, 0.0)
        third = [r[:, 128:256] for r in rows]
        folded = jnp.concatenate(
            [jnp.where(left, third[n], third[n + HALF // 8]) for n in range(HALF // 8)], 0
        )
        out_ref[j, CAP:PACK, :] = jnp.where(row_low < count, folded, 0.0)
        return start + count

    lax.fori_loop(0, COLS, one, jnp.int32(0))


def coeff_kernel(counts_ref, x_ref, out_ref, buf_ref):
    load_transposed(x_ref, buf_ref)
    write_slots(counts_ref, buf_ref, out_ref)


def alpha_kernel(counts_ref, blocks_ref, types_ref, x_ref, table_ref, out_ref, buf_ref, a_ref, hi_ref, lo_ref):
    load_transposed(x_ref, buf_ref)
    blocks = NA // BLK
    for b in range(blocks):
        hi, lo = split(buf_ref[BLK * b:BLK * b + BLK, :])
        for half in range(2):
            at = slice(128 * b + BLK * half, 128 * b + BLK * half + BLK)
            hi_ref[at, :] = hi
            lo_ref[at, :] = lo

    def place(i, carry):
        for k in range(blocks):
            col = pl.multiple_of(blocks_ref[i, k] * 128, 128)
            row = pl.multiple_of(i * BLK, BLK)
            a_ref[pl.ds(row, BLK), pl.ds(col, 128)] = table_ref[types_ref[i, k]]
        return carry

    lax.fori_loop(0, blocks, place, 0)
    for r in range(4):
        rows = slice(256 * r, 256 * r + 256)
        a = a_ref[rows, :]
        buf_ref[rows, :] = jnp.dot(a, hi_ref[...], preferred_element_type=f32) + jnp.dot(
            a, lo_ref[...], preferred_element_type=f32
        )
    write_slots(counts_ref, buf_ref, out_ref)


def swap(x):
    return pltpu.roll(x, BLK, 1)


def unpack(ref, senders, z_ref):
    left = left_half((CAP, 128))
    left_low = left_half((HALF, 128))

    def one(j, carry):
        main = ref[j, 0:CAP, :]
        low = ref[j, CAP:PACK, :]
        main_r = swap(main)
        low_r = swap(low)
        parts = (
            jnp.where(left, main, main_r),
            jnp.where(left, main_r, main),
            jnp.concatenate([jnp.where(left_low, low, low_r), jnp.where(left_low, low_r, low)], 0),
        )
        for n in range(3):
            hi, lo = split(parts[n])
            z_ref[3 * j + n] = jnp.concatenate([hi, lo], 1)
        return carry

    lax.fori_loop(0, senders, one, 0)
    z_ref[3 * senders] = jnp.zeros((CAP, 256), bf16)


def plan_kernel(blocks_ref, types_ref, words_ref, lists_ref, totals_ref, entry_ref, counts_ref, smem_ref, sem):
    entry_ref[...] = jnp.full((16, 128), 1 << 20, jnp.int32)
    entry_ref[0:DEPTH, 0:BLOCKS] = blocks_ref[...]
    entries = entry_ref[...]
    entry_ref[...] = jnp.zeros((16, 128), jnp.int32)
    entry_ref[0:DEPTH, 0:BLOCKS] = types_ref[...]
    types = entry_ref[...]
    row = lax.broadcasted_iota(jnp.int32, (16, 128), 0)
    counts_ref[...] = jnp.zeros((8, 128), jnp.int32)
    for q in range(3):
        low, high = BOUNDS[q], BOUNDS[q + 1]
        held = jnp.where((entries >= low) & (entries < high), 1, 0)
        word = (types << 8) | (entries - low)
        rank = jnp.zeros((1, 128), jnp.int32)
        ordered = jnp.full((16, 128), high - low, jnp.int32)
        for k in range(DEPTH):
            here = (row == rank) & (held[k:k + 1] > 0)
            ordered = jnp.where(here, word[k:k + 1], ordered)
            rank = rank + held[k:k + 1]
        words_ref[16 * q:16 * q + 16, :] = ordered
        counts_ref[q:q + 1, :] = (rank + GROUP - 1) // GROUP
    copy = pltpu.make_async_copy(counts_ref, smem_ref, sem)
    copy.start()
    copy.wait()

    def add(m, ends):
        ends = list(ends)
        for q in range(3):
            for i in range(DEPTH // GROUP):
                lists_ref[ends[q] + i] = m * 4 + i
            ends[q] = ends[q] + smem_ref[q, m]
        return tuple(ends)

    ends = lax.fori_loop(0, BLOCKS, add, tuple(jnp.int32(LIST * q) for q in range(3)), unroll=4)
    for q in range(3):
        for i in range(UNROLL):
            lists_ref[ends[q] + i] = BLOCKS * 4
        totals_ref[q] = (ends[q] - LIST * q + UNROLL - 1) // UNROLL


def accumulate(q, words_ref, lists_ref, totals_ref, z_ref, table_ref, acc_ref):
    pick = left_half((CAP, 256)) | (lax.broadcasted_iota(jnp.int32, (CAP, 256), 1) // BLK == 2)

    def batch(n, carry):
        for g in range(UNROLL):
            item = lists_ref[LIST * q + n * UNROLL + g]
            m = item >> 2
            at = 2048 * q + (item & 3) * 512 + m
            hi, lo, w = [], [], []
            for i in range(0, GROUP, 2):
                w0 = words_ref[at + 128 * i]
                w1 = words_ref[at + 128 * i + 128]
                pair = jnp.where(pick, z_ref[w0 & 255], z_ref[w1 & 255])
                hi.append(pair[:, 0:128])
                lo.append(pair[:, 128:256])
                w += [table_ref[w0 >> 8], table_ref[w1 >> 8]]
            lhs = jnp.concatenate([jnp.concatenate(hi, 1), jnp.concatenate(lo, 1)], 0)
            both = jnp.dot(lhs, jnp.concatenate(w, 0), preferred_element_type=f32)
            acc_ref[m] = acc_ref[m] + (both[0:CAP] + both[CAP:])
        return carry

    lax.fori_loop(0, totals_ref[q], batch, 0)


def zero(acc_ref):
    def one(m, carry):
        acc_ref[m] = jnp.zeros((CAP, 128), f32)
        return carry

    lax.fori_loop(0, BLOCKS + 1, one, 0)


def folded(acc_ref, pair, left):
    a = acc_ref[2 * pair]
    b = acc_ref[2 * pair + 1]
    return jnp.where(left, a + swap(a), b + swap(b))


def own_kernel(words_ref, lists_ref, totals_ref, own_ref, table_ref, acc_ref, x_ref):
    zero(acc_ref)
    unpack(own_ref, COLS, x_ref)
    accumulate(0, words_ref, lists_ref, totals_ref, x_ref, table_ref, acc_ref)


def first_kernel(words_ref, lists_ref, totals_ref, partner_ref, table_ref, prior_hbm, out_ref, x_ref, acc_ref, sem):
    copy = pltpu.make_async_copy(prior_hbm, acc_ref, sem)
    copy.start()
    unpack(partner_ref, FIRST, x_ref)
    copy.wait()
    accumulate(1, words_ref, lists_ref, totals_ref, x_ref, table_ref, acc_ref)
    left = left_half((CAP, 128))

    def one(p, carry):
        out_ref[:, pl.ds(pl.multiple_of(p * 128, 128), 128)] = folded(acc_ref, p, left)
        return carry

    lax.fori_loop(0, BLOCKS // 2, one, 0)


def last_kernel(
    words_ref, lists_ref, totals_ref, partner_ref, table_ref, prior_hbm, alpha_hbm, out_hbm,
    x_ref, acc_ref, prior_ref, alpha_ref, out_ref, sems, out_sems,
):
    prior_copy = pltpu.make_async_copy(prior_hbm, prior_ref, sems.at[0])
    alpha_copy = pltpu.make_async_copy(alpha_hbm, alpha_ref, sems.at[1])
    prior_copy.start()
    alpha_copy.start()
    zero(acc_ref)
    unpack(partner_ref, COLS - FIRST, x_ref)
    accumulate(2, words_ref, lists_ref, totals_ref, x_ref, table_ref, acc_ref)
    prior_copy.wait()
    alpha_copy.wait()
    left = left_half((CAP, 128))

    def triple(u, carry):
        a_main, a_low = alpha_ref[2 * u, 0:CAP, :], alpha_ref[2 * u, CAP:PACK, :]
        b_main, b_low = alpha_ref[2 * u + 1, 0:CAP, :], alpha_ref[2 * u + 1, CAP:PACK, :]
        b_main_r = swap(b_main)
        alphas = (
            a_main,
            jnp.where(left, jnp.concatenate([a_low, swap(a_low)], 0), b_main_r),
            jnp.where(left, b_main_r, jnp.concatenate([swap(b_low), b_low], 0)),
        )
        for n in range(3):
            col = pl.ds(pl.multiple_of(u * 384 + 128 * n, 128), 128)
            out_ref[:, col] = alphas[n] + (prior_ref[:, col] + folded(acc_ref, 3 * u + n, left))
        return carry

    copies = []
    for part in range(4):
        lax.fori_loop(4 * part, 4 * part + 4, triple, 0)
        cols = slice(1536 * part, 1536 * part + 1536)
        copy = pltpu.make_async_copy(out_ref.at[:, cols], out_hbm.at[:, cols], out_sems.at[part])
        copy.start()
        copies.append(copy)
    for copy in copies:
        copy.wait()


def smem():
    return pl.BlockSpec(memory_space=pltpu.SMEM)


def vmem():
    return pl.BlockSpec(memory_space=pltpu.VMEM)


def hbm():
    return pl.BlockSpec(memory_space=pltpu.HBM)


def split_table(table):
    tiles = table.reshape(table.shape[0], BLK, BLK)
    hi = lax.reduce_precision(tiles, 8, 7)
    return jnp.concatenate([hi, tiles - hi], 2).astype(bf16)


def on_device(coeffs_t, alpha_table, alpha_blocks, alpha_types, beta_table, beta_blocks, beta_types, row_counts):
    slots = jax.ShapeDtypeStruct((COLS, PACK, 128), f32)
    coeff_slots = pl.pallas_call(
        coeff_kernel,
        in_specs=[smem(), vmem()],
        out_specs=vmem(),
        out_shape=slots,
        scratch_shapes=[pltpu.VMEM((ROWS, 256), f32)],
        name="coeff_slots",
    )(row_counts, coeffs_t)
    alpha_slots = pl.pallas_call(
        alpha_kernel,
        in_specs=[smem(), smem(), smem(), vmem(), vmem()],
        out_specs=vmem(),
        out_shape=slots,
        scratch_shapes=[
            pltpu.VMEM((ROWS, 256), f32),
            pltpu.VMEM((NA, 2 * NA), bf16),
            pltpu.VMEM((2 * NA, 256), bf16),
            pltpu.VMEM((2 * NA, 256), bf16),
        ],
        name="alpha_slots",
    )(row_counts, alpha_blocks, alpha_types, coeffs_t, split_table(alpha_table))
    words, lists, totals = pl.pallas_call(
        plan_kernel,
        in_specs=[vmem(), vmem()],
        out_specs=[vmem(), smem(), smem()],
        out_shape=[
            jax.ShapeDtypeStruct((48, 128), jnp.int32),
            jax.ShapeDtypeStruct((3 * LIST,), jnp.int32),
            jax.ShapeDtypeStruct((3,), jnp.int32),
        ],
        scratch_shapes=[
            pltpu.VMEM((16, 128), jnp.int32),
            pltpu.VMEM((8, 128), jnp.int32),
            pltpu.SMEM((8, 128), jnp.int32),
            pltpu.SemaphoreType.DMA,
        ],
        name="beta_plan",
    )(beta_blocks.T, beta_types.T)
    words = words.reshape(-1)
    tiles = split_table(beta_table)
    own = lax.all_to_all(coeff_slots, "col", split_axis=0, concat_axis=0, tiled=True)
    own, alpha_slots, tiles, words, lists, totals = lax.optimization_barrier(
        (own, alpha_slots, tiles, words, lists, totals)
    )
    route = [(i, i ^ 1) for i in range(8)]
    partner_first = lax.ppermute(own[:FIRST], "cls", route)
    alpha = lax.all_to_all(alpha_slots, "col", split_axis=0, concat_axis=0, tiled=True)
    acc_shape = (BLOCKS + 1, CAP, 128)
    acc = pl.pallas_call(
        own_kernel,
        in_specs=[smem(), smem(), smem(), vmem(), vmem()],
        out_specs=vmem(),
        out_shape=jax.ShapeDtypeStruct(acc_shape, f32),
        scratch_shapes=[pltpu.VMEM((3 * COLS + 1, CAP, 256), bf16)],
        name="beta_own",
    )(words, lists, totals, own, tiles)
    rest, acc = lax.optimization_barrier((own[FIRST:], acc))
    partner_last = lax.ppermute(rest, "cls", route)
    prior = pl.pallas_call(
        first_kernel,
        in_specs=[smem(), smem(), smem(), vmem(), vmem(), hbm()],
        out_specs=vmem(),
        out_shape=jax.ShapeDtypeStruct((CAP, BLOCKS * BLK), f32),
        scratch_shapes=[
            pltpu.VMEM((3 * FIRST + 1, CAP, 256), bf16),
            pltpu.VMEM(acc_shape, f32),
            pltpu.SemaphoreType.DMA,
        ],
        name="beta_first",
    )(words, lists, totals, partner_first, tiles, acc)
    return pl.pallas_call(
        last_kernel,
        in_specs=[smem(), smem(), smem(), vmem(), vmem(), hbm(), hbm()],
        out_specs=hbm(),
        out_shape=jax.ShapeDtypeStruct((CAP, BLOCKS * BLK), f32),
        scratch_shapes=[
            pltpu.VMEM((3 * (COLS - FIRST) + 1, CAP, 256), bf16),
            pltpu.VMEM(acc_shape, f32),
            pltpu.VMEM((CAP, BLOCKS * BLK), f32),
            pltpu.VMEM((COLS, PACK, 128), f32),
            pltpu.VMEM((CAP, BLOCKS * BLK), f32),
            pltpu.SemaphoreType.DMA((2,)),
            pltpu.SemaphoreType.DMA((4,)),
        ],
        name="beta_last",
    )(words, lists, totals, partner_last, tiles, prior, alpha)


def solution(mesh):
    return jax.shard_map(
        on_device,
        mesh=mesh,
        in_specs=(P(("cls", "col"), None), P(), P(), P(), P(), P("cls", None), P("cls", None), P()),
        out_specs=P("col", "cls"),
        check_vma=False,
    )
```

```python
import jax
import jax.numpy as jnp
from jax import lax
from jax.experimental import pallas as pl
from jax.experimental.pallas import tpu as pltpu
from jax.sharding import PartitionSpec as P

f32 = jnp.float32
bf16 = jnp.bfloat16

NA = 1024
BLK = 64
COLS = 32
CAP = 48
HALF = CAP // 2
PACK = CAP + HALF
BLOCKS = 96
DEPTH = 12
PARTS = ((0, 32, 0), (32, 16, 48))
SPLIT = 48
TRIP = 12
ROWS = NA + CAP + 8


def split(x):
    hi = x.astype(bf16)
    return hi, (x - hi.astype(f32)).astype(bf16)


def left_half(shape):
    return lax.broadcasted_iota(jnp.int32, shape, len(shape) - 1) < BLK


def load_transposed(x_ref, buf_ref):
    for c in range(NA // 128):
        cols = slice(128 * c, 128 * c + 128)
        last = x_ref[128:192, cols]
        buf_ref[cols, 0:128] = x_ref[0:128, cols].T
        buf_ref[cols, 128:256] = jnp.concatenate([last, last], 0).T


def write_slots(counts_ref, buf_ref, out_ref):
    buf_ref[NA:ROWS, :] = jnp.zeros((ROWS - NA, 256), f32)
    left = left_half((8, 128))
    sub = lax.broadcasted_iota(jnp.int32, (8, 256), 0)

    def one(j, start):
        count = counts_ref[j]
        base = pl.multiple_of((start // 8) * 8, 8)
        shift = 8 - (start - base)
        turned = [pltpu.roll(buf_ref[pl.ds(base + 8 * n, 8), :], shift & 7, 0) for n in range(CAP // 8 + 1)]
        main, third = [], []
        for n in range(CAP // 8):
            rows = jnp.where(sub < shift, turned[n], turned[n + 1])
            rows = jnp.where(sub < count - 8 * n, rows, 0.0)
            main.append(rows[:, 0:128])
            third.append(rows[:, 128:256])
        for part in range(2):
            first, size, at = PARTS[part]
            n0, n1 = first // 8, size // 8
            half = n1 // 2
            low = [jnp.where(left, third[n0 + n], third[n0 + half + n]) for n in range(half)]
            out_ref[j, at:at + size, :] = jnp.concatenate(main[n0:n0 + n1], 0)
            out_ref[j, at + size:at + size + size // 2, :] = jnp.concatenate(low, 0) if half > 1 else low[0]
        return start + count

    lax.fori_loop(0, COLS, one, jnp.int32(0))


def coeff_kernel(counts_ref, x_ref, out_ref, buf_ref):
    load_transposed(x_ref, buf_ref)
    write_slots(counts_ref, buf_ref, out_ref)


def alpha_kernel(counts_ref, blocks_ref, types_ref, x_ref, table_ref, out_ref, buf_ref, a_ref, hi_ref, lo_ref):
    load_transposed(x_ref, buf_ref)
    blocks = NA // BLK
    for b in range(blocks):
        hi, lo = split(buf_ref[BLK * b:BLK * b + BLK, :])
        for half in range(2):
            at = slice(128 * b + BLK * half, 128 * b + BLK * half + BLK)
            hi_ref[at, :] = hi
            lo_ref[at, :] = lo

    def place(i, carry):
        for k in range(blocks):
            col = pl.multiple_of(blocks_ref[i, k] * 128, 128)
            row = pl.multiple_of(i * BLK, BLK)
            a_ref[pl.ds(row, BLK), pl.ds(col, 128)] = table_ref[types_ref[i, k]]
        return carry

    lax.fori_loop(0, blocks, place, 0)
    for r in range(4):
        rows = slice(256 * r, 256 * r + 256)
        a = a_ref[rows, :]
        buf_ref[rows, :] = jnp.dot(a, hi_ref[...], preferred_element_type=f32) + jnp.dot(
            a, lo_ref[...], preferred_element_type=f32
        )
    write_slots(counts_ref, buf_ref, out_ref)


def swap(x):
    return pltpu.roll(x, BLK, 1)


def fields(ref, j, size, at):
    main = ref[j, at:at + size, :]
    low = ref[j, at + size:at + size + size // 2, :]
    return main, swap(main), low, swap(low)


def unpack(ref, size, at, z_ref, base):
    left = left_half((size, 128))
    left_low = left_half((size // 2, 128))

    def one(j, carry):
        main, main_r, low, low_r = fields(ref, j, size, at)
        parts = (
            jnp.where(left, main, main_r),
            jnp.where(left, main_r, main),
            jnp.concatenate([jnp.where(left_low, low, low_r), jnp.where(left_low, low_r, low)], 0),
        )
        for n in range(3):
            hi, lo = split(parts[n])
            z_ref[base + 3 * j + n] = jnp.concatenate([hi, lo], 1)
        return carry

    lax.fori_loop(0, COLS, one, 0, unroll=2)


def own_kernel(own_ref, za_ref, zb_ref):
    for (first, size, at), z_ref in zip(PARTS, (za_ref, zb_ref)):
        unpack(own_ref, size, at, z_ref, 0)


def product(blocks_ref, types_ref, z_ref, table_ref, size, store):
    pick = left_half((size, 256)) | (lax.broadcasted_iota(jnp.int32, (size, 256), 1) // BLK == 2)
    left = left_half((size, 128))

    def block(m):
        hi, lo, w = [], [], []
        for k in range(0, DEPTH, 2):
            pair = jnp.where(pick, z_ref[blocks_ref[k, m]], z_ref[blocks_ref[k + 1, m]])
            hi.append(pair[:, 0:128])
            lo.append(pair[:, 128:256])
            w.append(table_ref[types_ref[k, m]])
            w.append(table_ref[types_ref[k + 1, m]])
        lhs = jnp.concatenate([jnp.concatenate(hi, 1), jnp.concatenate(lo, 1)], 0)
        both = jnp.dot(lhs, jnp.concatenate(w, 0), preferred_element_type=f32)
        both = both[0:size] + both[size:]
        return both + swap(both)

    def trip(n, carry):
        for i in range(TRIP):
            p = n * TRIP + i
            col = pl.ds(pl.multiple_of(p * 128, 128), 128)
            store(col, jnp.where(left, block(2 * p), block(2 * p + 1)))
        return carry

    lax.fori_loop(0, BLOCKS // (2 * TRIP), trip, 0)


def first_kernel(blocks_ref, types_ref, own_hbm, partner_hbm, table_ref, out_ref, z_ref, partner_ref, sems):
    size = PARTS[0][1]
    own_copy = pltpu.make_async_copy(own_hbm, z_ref.at[0:BLOCKS], sems.at[0])
    partner_copy = pltpu.make_async_copy(partner_hbm, partner_ref, sems.at[1])
    partner_copy.start()
    own_copy.start()
    partner_copy.wait()
    unpack(partner_ref, size, 0, z_ref, BLOCKS)
    own_copy.wait()

    def store(col, value):
        out_ref[:, col] = value

    product(blocks_ref, types_ref, z_ref, table_ref, size, store)


def last_kernel(
    blocks_ref, types_ref, own_hbm, partner_ref, table_ref, first_hbm, alpha_hbm, out_hbm,
    z_ref, alpha_ref, out_ref, sems, out_sems,
):
    (_, size_a, at_a), (start, size, at_b) = PARTS
    own_copy = pltpu.make_async_copy(own_hbm, z_ref.at[0:BLOCKS], sems.at[0])
    first_copy = pltpu.make_async_copy(first_hbm, out_ref.at[0:start, :], sems.at[1])
    alpha_copy = pltpu.make_async_copy(alpha_hbm, alpha_ref, sems.at[2])
    own_copy.start()
    first_copy.start()
    alpha_copy.start()
    unpack(partner_ref, size, 0, z_ref, BLOCKS)
    own_copy.wait()

    def store(col, value):
        out_ref[start:CAP, col] = value

    product(blocks_ref, types_ref, z_ref, table_ref, size, store)
    first_copy.wait()
    alpha_copy.wait()

    def triple(u, carry):
        for rows, length, at in ((0, size_a, at_a), (start, size, at_b)):
            left = left_half((length, 128))
            a_main, _, a_low, a_low_r = fields(alpha_ref, 2 * u, length, at)
            _, b_main_r, b_low, b_low_r = fields(alpha_ref, 2 * u + 1, length, at)
            alphas = (
                a_main,
                jnp.where(left, jnp.concatenate([a_low, a_low_r], 0), b_main_r),
                jnp.where(left, b_main_r, jnp.concatenate([b_low_r, b_low], 0)),
            )
            for n in range(3):
                col = pl.ds(pl.multiple_of(u * 384 + 128 * n, 128), 128)
                out_ref[rows:rows + length, col] = alphas[n] + out_ref[rows:rows + length, col]
        return carry

    copies = []
    for part in range(4):
        lax.fori_loop(4 * part, 4 * part + 4, triple, 0, unroll=2)
        cols = slice(1536 * part, 1536 * part + 1536)
        copy = pltpu.make_async_copy(out_ref.at[:, cols], out_hbm.at[:, cols], out_sems.at[part])
        copy.start()
        copies.append(copy)
    for copy in copies:
        copy.wait()


def in_vmem(x):
    return pltpu.with_memory_space_constraint(x, pltpu.VMEM)


def smem():
    return pl.BlockSpec(memory_space=pltpu.SMEM)


def vmem():
    return pl.BlockSpec(memory_space=pltpu.VMEM)


def hbm():
    return pl.BlockSpec(memory_space=pl.ANY)


def split_table(table):
    tiles = table.reshape(table.shape[0], BLK, BLK)
    hi = lax.reduce_precision(tiles, 8, 7)
    return jnp.concatenate([hi, tiles - hi], 2).astype(bf16)


def on_device(coeffs_t, alpha_table, alpha_blocks, alpha_types, beta_table, beta_blocks, beta_types, row_counts):
    slots = jax.ShapeDtypeStruct((COLS, PACK, 128), f32)
    coeff_slots = pl.pallas_call(
        coeff_kernel,
        in_specs=[smem(), vmem()],
        out_specs=vmem(),
        out_shape=slots,
        scratch_shapes=[pltpu.VMEM((ROWS, 256), f32)],
        name="coeff_slots",
    )(row_counts, coeffs_t)
    alpha_slots = pl.pallas_call(
        alpha_kernel,
        in_specs=[smem(), smem(), smem(), vmem(), vmem()],
        out_specs=vmem(),
        out_shape=slots,
        scratch_shapes=[
            pltpu.VMEM((ROWS, 256), f32),
            pltpu.VMEM((NA, 2 * NA), bf16),
            pltpu.VMEM((2 * NA, 256), bf16),
            pltpu.VMEM((2 * NA, 256), bf16),
        ],
        name="alpha_slots",
    )(row_counts, alpha_blocks, alpha_types, coeffs_t, split_table(alpha_table))
    tiles = split_table(beta_table)
    own = lax.all_to_all(coeff_slots, "col", split_axis=0, concat_axis=0, tiled=True)
    own, alpha_slots, tiles = lax.optimization_barrier((own, alpha_slots, tiles))
    tiles = in_vmem(tiles)
    route = [(i, i ^ 1) for i in range(8)]
    partner_first = lax.ppermute(own[:, :SPLIT], "cls", route)
    alpha = lax.all_to_all(alpha_slots, "col", split_axis=0, concat_axis=0, tiled=True)
    sizes = [PARTS[0][1], PARTS[1][1]]
    own_first, own_last = pl.pallas_call(
        own_kernel,
        in_specs=[vmem()],
        out_specs=[vmem(), vmem()],
        out_shape=[jax.ShapeDtypeStruct((BLOCKS, size, 256), bf16) for size in sizes],
        name="own_split",
    )(own)
    rest, own_first, own_last = lax.optimization_barrier((own[:, SPLIT:], own_first, own_last))
    partner_last = lax.ppermute(rest, "cls", route)
    blocks, types = beta_blocks.T, beta_types.T
    first = pl.pallas_call(
        first_kernel,
        in_specs=[smem(), smem(), hbm(), hbm(), vmem()],
        out_specs=vmem(),
        out_shape=jax.ShapeDtypeStruct((sizes[0], BLOCKS * BLK), f32),
        scratch_shapes=[
            pltpu.VMEM((2 * BLOCKS, sizes[0], 256), bf16),
            pltpu.VMEM((COLS, SPLIT, 128), f32),
            pltpu.SemaphoreType.DMA((2,)),
        ],
        name="beta_first",
    )(blocks, types, own_first, partner_first, tiles)
    return pl.pallas_call(
        last_kernel,
        in_specs=[smem(), smem(), hbm(), vmem(), vmem(), hbm(), hbm()],
        out_specs=hbm(),
        out_shape=jax.ShapeDtypeStruct((CAP, BLOCKS * BLK), f32),
        scratch_shapes=[
            pltpu.VMEM((2 * BLOCKS, sizes[1], 256), bf16),
            pltpu.VMEM((COLS, PACK, 128), f32),
            pltpu.VMEM((CAP, BLOCKS * BLK), f32),
            pltpu.SemaphoreType.DMA((3,)),
            pltpu.SemaphoreType.DMA((4,)),
        ],
        name="beta_last",
    )(blocks, types, own_last, in_vmem(partner_last), tiles, first, alpha)


def solution(mesh):
    return jax.shard_map(
        on_device,
        mesh=mesh,
        in_specs=(P(("cls", "col"), None), P(), P(), P(), P(), P("cls", None), P("cls", None), P()),
        out_specs=P("col", "cls"),
        check_vma=False,
    )
```

```python
import jax
import jax.numpy as jnp
from jax import lax
from jax.experimental import pallas as pl
from jax.experimental.pallas import tpu as pltpu
from jax.sharding import PartitionSpec as P

f32 = jnp.float32
bf16 = jnp.bfloat16

NA = 1024
BLK = 64
COLS = 32
CAP = 48
LOCAL = 192
HALF = CAP // 2
PACK = CAP + HALF
BLOCKS = 96
DEPTH = 12
PARTS = ((0, 32, 0), (32, 16, 48))
PIECES = 4
SPLIT = 48
TRIP = 24
ROWS = NA + CAP + 8


def split(x):
    hi = x.astype(bf16)
    return hi, (x - hi.astype(f32)).astype(bf16)


def left_half(shape):
    return lax.broadcasted_iota(jnp.int32, shape, len(shape) - 1) < BLK


def transpose_columns(x_ref, buf_ref, chunks):
    for c in chunks:
        cols = slice(128 * c, 128 * c + 128)
        last = x_ref[128:192, cols]
        buf_ref[cols, 0:128] = x_ref[0:128, cols].T
        buf_ref[cols, 128:256] = jnp.concatenate([last, last], 0).T


def write_slots(counts_ref, buf_ref, out_ref, done=None):
    buf_ref[NA:ROWS, :] = jnp.zeros((ROWS - NA, 256), f32)
    left = left_half((8, 128))
    sub = lax.broadcasted_iota(jnp.int32, (8, 256), 0)

    def one(j, start):
        count = counts_ref[j]
        base = pl.multiple_of((start // 8) * 8, 8)
        shift = 8 - (start - base)
        turned = [pltpu.roll(buf_ref[pl.ds(base + 8 * n, 8), :], shift & 7, 0) for n in range(CAP // 8 + 1)]
        main, third = [], []
        for n in range(CAP // 8):
            rows = jnp.where(sub < shift, turned[n], turned[n + 1])
            rows = jnp.where(sub < count - 8 * n, rows, 0.0)
            main.append(rows[:, 0:128])
            third.append(rows[:, 128:256])
        for part in range(2):
            first, size, at = PARTS[part]
            n0, n1 = first // 8, size // 8
            half = n1 // 2
            low = [jnp.where(left, third[n0 + n], third[n0 + half + n]) for n in range(half)]
            out_ref[j, at:at + size, :] = jnp.concatenate(main[n0:n0 + n1], 0)
            out_ref[j, at + size:at + size + size // 2, :] = jnp.concatenate(low, 0) if half > 1 else low[0]
        return start + count

    start = jnp.int32(0)
    for piece in range(PIECES):
        each = COLS // PIECES
        start = lax.fori_loop(each * piece, each * piece + each, one, start)
        if done is not None:
            done(piece)


def coeff_kernel(counts_ref, x_hbm, out_hbm, x_ref, out_ref, buf_ref, in_sems, out_sems):
    width, each = NA // 2, COLS // PIECES
    loads = []
    for piece in range(2):
        cols = slice(width * piece, width * piece + width)
        loads.append(pltpu.make_async_copy(x_hbm.at[:, cols], x_ref.at[:, cols], in_sems.at[piece]))
        loads[-1].start()
    for piece in range(2):
        loads[piece].wait()
        transpose_columns(x_ref, buf_ref, range(width // 128 * piece, width // 128 * (piece + 1)))
    stores = []

    def done(piece):
        rows = slice(each * piece, each * piece + each)
        stores.append(pltpu.make_async_copy(out_ref.at[rows], out_hbm.at[rows], out_sems.at[piece]))
        stores[-1].start()

    write_slots(counts_ref, buf_ref, out_ref, done)
    for store in stores:
        store.wait()


def alpha_kernel(counts_ref, blocks_ref, types_ref, x_ref, table_ref, out_ref, buf_ref, a_ref, hi_ref, lo_ref):
    transpose_columns(x_ref, buf_ref, range(NA // 128))
    blocks = NA // BLK
    for b in range(blocks):
        hi, lo = split(buf_ref[BLK * b:BLK * b + BLK, :])
        for half in range(2):
            at = slice(128 * b + BLK * half, 128 * b + BLK * half + BLK)
            hi_ref[at, :] = hi
            lo_ref[at, :] = lo

    def place(i, carry):
        for k in range(blocks):
            col = pl.multiple_of(blocks_ref[i, k] * 128, 128)
            row = pl.multiple_of(i * BLK, BLK)
            a_ref[pl.ds(row, BLK), pl.ds(col, 128)] = table_ref[types_ref[i, k]]
        return carry

    lax.fori_loop(0, blocks, place, 0)
    for r in range(4):
        rows = slice(256 * r, 256 * r + 256)
        a = a_ref[rows, :]
        buf_ref[rows, :] = jnp.dot(a, hi_ref[...], preferred_element_type=f32) + jnp.dot(
            a, lo_ref[...], preferred_element_type=f32
        )
    write_slots(counts_ref, buf_ref, out_ref)


def swap(x):
    return pltpu.roll(x, BLK, 1)


def fields(ref, j, size, at):
    main = ref[j, at:at + size, :]
    low = ref[j, at + size:at + size + size // 2, :]
    return main, swap(main), low, swap(low)


def unpack(ref, size, at, z_ref, base):
    left = left_half((size, 128))
    left_low = left_half((size // 2, 128))

    def one(j, carry):
        main, main_r, low, low_r = fields(ref, j, size, at)
        parts = (
            jnp.where(left, main, main_r),
            jnp.where(left, main_r, main),
            jnp.concatenate([jnp.where(left_low, low, low_r), jnp.where(left_low, low_r, low)], 0),
        )
        for n in range(3):
            hi, lo = split(parts[n])
            z_ref[base + 3 * j + n] = jnp.concatenate([hi, lo], 1)
        return carry

    lax.fori_loop(0, COLS, one, 0, unroll=2)


def own_kernel(own_ref, za_ref, zb_ref):
    for (first, size, at), z_ref in zip(PARTS, (za_ref, zb_ref)):
        unpack(own_ref, size, at, z_ref, 0)


def product(blocks_ref, types_ref, z_ref, table_ref, size, store):
    pick = left_half((size, 256)) | (lax.broadcasted_iota(jnp.int32, (size, 256), 1) // BLK == 2)
    left = left_half((size, 128))

    def block(m):
        hi, lo, w = [], [], []
        for k in range(0, DEPTH, 2):
            pair = jnp.where(pick, z_ref[blocks_ref[k, m]], z_ref[blocks_ref[k + 1, m]])
            hi.append(pair[:, 0:128])
            lo.append(pair[:, 128:256])
            w.append(table_ref[types_ref[k, m]])
            w.append(table_ref[types_ref[k + 1, m]])
        lhs = jnp.concatenate([jnp.concatenate(hi, 1), jnp.concatenate(lo, 1)], 0)
        both = jnp.dot(lhs, jnp.concatenate(w, 0), preferred_element_type=f32)
        both = both[0:size] + both[size:]
        return both + swap(both)

    def trip(n, carry):
        for i in range(TRIP):
            p = n * TRIP + i
            col = pl.ds(pl.multiple_of(p * 128, 128), 128)
            store(col, jnp.where(left, block(2 * p), block(2 * p + 1)))
        return carry

    lax.fori_loop(0, BLOCKS // (2 * TRIP), trip, 0)


def first_kernel(blocks_ref, types_ref, own_hbm, partner_ref, table_ref, out_ref, z_ref, sem):
    size = PARTS[0][1]
    own_copy = pltpu.make_async_copy(own_hbm, z_ref.at[0:BLOCKS], sem)
    own_copy.start()
    unpack(partner_ref, size, 0, z_ref, BLOCKS)
    own_copy.wait()

    def store(col, value):
        out_ref[:, col] = value

    product(blocks_ref, types_ref, z_ref, table_ref, size, store)


def last_kernel(
    blocks_ref, types_ref, own_hbm, partner_ref, table_ref, first_hbm, alpha_ref, out_hbm,
    z_ref, out_ref, sems, out_sems,
):
    (_, size_a, at_a), (start, size, at_b) = PARTS
    own_copy = pltpu.make_async_copy(own_hbm, z_ref.at[0:BLOCKS], sems.at[0])
    first_copy = pltpu.make_async_copy(first_hbm, out_ref.at[0:start, :], sems.at[1])
    own_copy.start()
    first_copy.start()
    unpack(partner_ref, size, 0, z_ref, BLOCKS)
    own_copy.wait()

    def store(col, value):
        out_ref[start:CAP, col] = value

    product(blocks_ref, types_ref, z_ref, table_ref, size, store)
    first_copy.wait()

    def triple(u, carry):
        for rows, length, at in ((0, size_a, at_a), (start, size, at_b)):
            left = left_half((length, 128))
            a_main, _, a_low, a_low_r = fields(alpha_ref, 2 * u, length, at)
            _, b_main_r, b_low, b_low_r = fields(alpha_ref, 2 * u + 1, length, at)
            alphas = (
                a_main,
                jnp.where(left, jnp.concatenate([a_low, a_low_r], 0), b_main_r),
                jnp.where(left, b_main_r, jnp.concatenate([b_low_r, b_low], 0)),
            )
            for n in range(3):
                col = pl.ds(pl.multiple_of(u * 384 + 128 * n, 128), 128)
                out_ref[rows:rows + length, col] = alphas[n] + out_ref[rows:rows + length, col]
        return carry

    copies = []
    for part in range(4):
        lax.fori_loop(4 * part, 4 * part + 4, triple, 0, unroll=2)
        cols = slice(1536 * part, 1536 * part + 1536)
        copy = pltpu.make_async_copy(out_ref.at[:, cols], out_hbm.at[:, cols], out_sems.at[part])
        copy.start()
        copies.append(copy)
    for copy in copies:
        copy.wait()


def in_vmem(x):
    return pltpu.with_memory_space_constraint(x, pltpu.VMEM)


def smem():
    return pl.BlockSpec(memory_space=pltpu.SMEM)


def vmem():
    return pl.BlockSpec(memory_space=pltpu.VMEM)


def hbm():
    return pl.BlockSpec(memory_space=pl.ANY)


def split_table(table):
    tiles = table.reshape(table.shape[0], BLK, BLK)
    hi = lax.reduce_precision(tiles, 8, 7)
    return jnp.concatenate([hi, tiles - hi], 2).astype(bf16)


def on_device(coeffs_t, alpha_table, alpha_blocks, alpha_types, beta_table, beta_blocks, beta_types, row_counts):
    slots = jax.ShapeDtypeStruct((COLS, PACK, 128), f32)
    coeff_slots = pl.pallas_call(
        coeff_kernel,
        in_specs=[smem(), hbm()],
        out_specs=hbm(),
        out_shape=slots,
        scratch_shapes=[
            pltpu.VMEM((LOCAL, NA), f32),
            pltpu.VMEM((COLS, PACK, 128), f32),
            pltpu.VMEM((ROWS, 256), f32),
            pltpu.SemaphoreType.DMA((2,)),
            pltpu.SemaphoreType.DMA((PIECES,)),
        ],
        name="coeff_slots",
    )(row_counts, coeffs_t)
    alpha_slots = pl.pallas_call(
        alpha_kernel,
        in_specs=[smem(), smem(), smem(), vmem(), vmem()],
        out_specs=vmem(),
        out_shape=slots,
        scratch_shapes=[
            pltpu.VMEM((ROWS, 256), f32),
            pltpu.VMEM((NA, 2 * NA), bf16),
            pltpu.VMEM((2 * NA, 256), bf16),
            pltpu.VMEM((2 * NA, 256), bf16),
        ],
        name="alpha_slots",
    )(row_counts, alpha_blocks, alpha_types, coeffs_t, split_table(alpha_table))
    tiles = split_table(beta_table)
    own = lax.all_to_all(coeff_slots, "col", split_axis=0, concat_axis=0, tiled=True)
    own, alpha_slots, tiles = lax.optimization_barrier((own, alpha_slots, tiles))
    tiles = in_vmem(tiles)
    route = [(i, i ^ 1) for i in range(8)]
    partner_first = lax.ppermute(in_vmem(own[:, :SPLIT]), "cls", route)
    alpha = lax.all_to_all(alpha_slots, "col", split_axis=0, concat_axis=0, tiled=True)
    sizes = [PARTS[0][1], PARTS[1][1]]
    own_first, own_last = pl.pallas_call(
        own_kernel,
        in_specs=[vmem()],
        out_specs=[vmem(), vmem()],
        out_shape=[jax.ShapeDtypeStruct((BLOCKS, size, 256), bf16) for size in sizes],
        name="own_split",
    )(own)
    rest, own_first, own_last = lax.optimization_barrier((own[:, SPLIT:], own_first, own_last))
    partner_last = lax.ppermute(rest, "cls", route)
    blocks, types = beta_blocks.T, beta_types.T
    first = pl.pallas_call(
        first_kernel,
        in_specs=[smem(), smem(), hbm(), vmem(), vmem()],
        out_specs=vmem(),
        out_shape=jax.ShapeDtypeStruct((sizes[0], BLOCKS * BLK), f32),
        scratch_shapes=[
            pltpu.VMEM((2 * BLOCKS, sizes[0], 256), bf16),
            pltpu.SemaphoreType.DMA,
        ],
        name="beta_first",
    )(blocks, types, own_first, in_vmem(partner_first), tiles)
    return pl.pallas_call(
        last_kernel,
        in_specs=[smem(), smem(), hbm(), vmem(), vmem(), hbm(), vmem()],
        out_specs=hbm(),
        out_shape=jax.ShapeDtypeStruct((CAP, BLOCKS * BLK), f32),
        scratch_shapes=[
            pltpu.VMEM((2 * BLOCKS, sizes[1], 256), bf16),
            pltpu.VMEM((CAP, BLOCKS * BLK), f32),
            pltpu.SemaphoreType.DMA((2,)),
            pltpu.SemaphoreType.DMA((4,)),
        ],
        name="beta_last",
    )(blocks, types, own_last, in_vmem(partner_last), tiles, first, in_vmem(alpha))


def solution(mesh):
    return jax.shard_map(
        on_device,
        mesh=mesh,
        in_specs=(P(("cls", "col"), None), P(), P(), P(), P(), P("cls", None), P("cls", None), P()),
        out_specs=P("col", "cls"),
        check_vma=False,
    )
```

```python
import jax
import jax.numpy as jnp
from jax import lax
from jax.experimental import pallas as pl
from jax.experimental.pallas import tpu as pltpu
from jax.sharding import PartitionSpec as P

f32 = jnp.float32
bf16 = jnp.bfloat16

NA = 1024
BLK = 64
COLS = 32
CAP = 48
LOCAL = 192
HALF = CAP // 2
PACK = CAP + HALF
BLOCKS = 96
DEPTH = 12
PARTS = ((0, 32, 0), (32, 16, 48))
PIECES = 4
SPLIT = 48
TRIP = 24
ROWS = NA + CAP + 8


def split(x):
    hi = x.astype(bf16)
    return hi, (x - hi.astype(f32)).astype(bf16)


def left_half(shape):
    return lax.broadcasted_iota(jnp.int32, shape, len(shape) - 1) < BLK


def transpose_pair(x_ref, buf_ref):
    for c in range(NA // 128):
        cols = slice(128 * c, 128 * c + 128)
        buf_ref[cols, 0:128] = x_ref[0:128, cols].T


def transpose_third(x_ref, buf_ref):
    for c in range(NA // 128):
        cols = slice(128 * c, 128 * c + 128)
        third = x_ref[128:LOCAL, cols]
        buf_ref[cols, 128:256] = jnp.concatenate([third, third], 0).T


def write_slots(counts_ref, buf_ref, out_ref, done=None):
    buf_ref[NA:ROWS, :] = jnp.zeros((ROWS - NA, 256), f32)
    left = left_half((8, 128))
    sub = lax.broadcasted_iota(jnp.int32, (8, 256), 0)

    def one(j, start):
        count = counts_ref[j]
        base = pl.multiple_of((start // 8) * 8, 8)
        shift = 8 - (start - base)
        turned = [pltpu.roll(buf_ref[pl.ds(base + 8 * n, 8), :], shift & 7, 0) for n in range(CAP // 8 + 1)]
        main, third = [], []
        for n in range(CAP // 8):
            rows = jnp.where(sub < shift, turned[n], turned[n + 1])
            rows = jnp.where(sub < count - 8 * n, rows, 0.0)
            main.append(rows[:, 0:128])
            third.append(rows[:, 128:256])
        for part in range(2):
            first, size, at = PARTS[part]
            n0, n1 = first // 8, size // 8
            half = n1 // 2
            low = [jnp.where(left, third[n0 + n], third[n0 + half + n]) for n in range(half)]
            out_ref[j, at:at + size, :] = jnp.concatenate(main[n0:n0 + n1], 0)
            out_ref[j, at + size:at + size + size // 2, :] = jnp.concatenate(low, 0) if half > 1 else low[0]
        return start + count

    start = jnp.int32(0)
    for piece in range(PIECES):
        each = COLS // PIECES
        start = lax.fori_loop(each * piece, each * piece + each, one, start)
        if done is not None:
            done(piece)


def coeff_kernel(counts_ref, x_hbm, out_hbm, x_ref, out_ref, buf_ref, in_sems, out_sems):
    each = COLS // PIECES
    loads = []
    for piece, rows in enumerate((slice(0, 128), slice(128, LOCAL))):
        loads.append(pltpu.make_async_copy(x_hbm.at[rows], x_ref.at[rows], in_sems.at[piece]))
        loads[-1].start()
    loads[0].wait()
    transpose_pair(x_ref, buf_ref)
    loads[1].wait()
    transpose_third(x_ref, buf_ref)
    stores = []

    def done(piece):
        rows = slice(each * piece, each * piece + each)
        stores.append(pltpu.make_async_copy(out_ref.at[rows], out_hbm.at[rows], out_sems.at[piece]))
        stores[-1].start()

    write_slots(counts_ref, buf_ref, out_ref, done)
    for store in stores:
        store.wait()


def alpha_kernel(counts_ref, blocks_ref, types_ref, x_ref, table_ref, out_ref, buf_ref, a_ref, hi_ref, lo_ref):
    transpose_pair(x_ref, buf_ref)
    transpose_third(x_ref, buf_ref)
    blocks = NA // BLK
    for b in range(blocks):
        hi, lo = split(buf_ref[BLK * b:BLK * b + BLK, :])
        for half in range(2):
            at = slice(128 * b + BLK * half, 128 * b + BLK * half + BLK)
            hi_ref[at, :] = hi
            lo_ref[at, :] = lo

    def place(i, carry):
        for k in range(blocks):
            col = pl.multiple_of(blocks_ref[i, k] * 128, 128)
            row = pl.multiple_of(i * BLK, BLK)
            a_ref[pl.ds(row, BLK), pl.ds(col, 128)] = table_ref[types_ref[i, k]]
        return carry

    lax.fori_loop(0, blocks, place, 0)
    for r in range(4):
        rows = slice(256 * r, 256 * r + 256)
        a = a_ref[rows, :]
        buf_ref[rows, :] = jnp.dot(a, hi_ref[...], preferred_element_type=f32) + jnp.dot(
            a, lo_ref[...], preferred_element_type=f32
        )
    write_slots(counts_ref, buf_ref, out_ref)


def swap(x):
    return pltpu.roll(x, BLK, 1)


def fields(ref, j, size, at):
    main = ref[j, at:at + size, :]
    low = ref[j, at + size:at + size + size // 2, :]
    return main, swap(main), low, swap(low)


def unpack(ref, size, at, z_ref, base):
    left = left_half((size, 128))
    left_low = left_half((size // 2, 128))

    def one(j, carry):
        main, main_r, low, low_r = fields(ref, j, size, at)
        parts = (
            jnp.where(left, main, main_r),
            jnp.where(left, main_r, main),
            jnp.concatenate([jnp.where(left_low, low, low_r), jnp.where(left_low, low_r, low)], 0),
        )
        for n in range(3):
            hi, lo = split(parts[n])
            z_ref[base + 3 * j + n] = jnp.concatenate([hi, lo], 1)
        return carry

    lax.fori_loop(0, COLS, one, 0, unroll=2)


def own_kernel(own_ref, za_ref, zb_ref):
    for (first, size, at), z_ref in zip(PARTS, (za_ref, zb_ref)):
        unpack(own_ref, size, at, z_ref, 0)


def product(blocks_ref, types_ref, z_ref, table_ref, size, store):
    pick = left_half((size, 256)) | (lax.broadcasted_iota(jnp.int32, (size, 256), 1) // BLK == 2)
    left = left_half((size, 128))

    def block(m):
        hi, lo, w = [], [], []
        for k in range(0, DEPTH, 2):
            pair = jnp.where(pick, z_ref[blocks_ref[k, m]], z_ref[blocks_ref[k + 1, m]])
            hi.append(pair[:, 0:128])
            lo.append(pair[:, 128:256])
            w.append(table_ref[types_ref[k, m]])
            w.append(table_ref[types_ref[k + 1, m]])
        lhs = jnp.concatenate([jnp.concatenate(hi, 1), jnp.concatenate(lo, 1)], 0)
        both = jnp.dot(lhs, jnp.concatenate(w, 0), preferred_element_type=f32)
        both = both[0:size] + both[size:]
        return both + swap(both)

    def trip(n, carry):
        for i in range(TRIP):
            p = n * TRIP + i
            col = pl.ds(pl.multiple_of(p * 128, 128), 128)
            store(col, jnp.where(left, block(2 * p), block(2 * p + 1)))
        return carry

    lax.fori_loop(0, BLOCKS // (2 * TRIP), trip, 0)


def first_kernel(blocks_ref, types_ref, own_hbm, partner_ref, table_hbm, out_ref, z_ref, table_ref, sems):
    size = PARTS[0][1]
    own_copy = pltpu.make_async_copy(own_hbm, z_ref.at[0:BLOCKS], sems.at[0])
    table_copy = pltpu.make_async_copy(table_hbm, table_ref, sems.at[1])
    own_copy.start()
    table_copy.start()
    unpack(partner_ref, size, 0, z_ref, BLOCKS)
    own_copy.wait()
    table_copy.wait()

    def store(col, value):
        out_ref[:, col] = value

    product(blocks_ref, types_ref, z_ref, table_ref, size, store)


def last_kernel(
    blocks_ref, types_ref, own_hbm, partner_ref, table_hbm, first_hbm, alpha_ref, out_hbm,
    z_ref, table_ref, out_ref, sems, out_sems,
):
    (_, size_a, at_a), (start, size, at_b) = PARTS
    own_copy = pltpu.make_async_copy(own_hbm, z_ref.at[0:BLOCKS], sems.at[0])
    first_copy = pltpu.make_async_copy(first_hbm, out_ref.at[0:start, :], sems.at[1])
    table_copy = pltpu.make_async_copy(table_hbm, table_ref, sems.at[2])
    own_copy.start()
    table_copy.start()
    first_copy.start()
    unpack(partner_ref, size, 0, z_ref, BLOCKS)
    own_copy.wait()
    table_copy.wait()

    def store(col, value):
        out_ref[start:CAP, col] = value

    product(blocks_ref, types_ref, z_ref, table_ref, size, store)
    first_copy.wait()

    def triple(u, carry):
        for rows, length, at in ((0, size_a, at_a), (start, size, at_b)):
            left = left_half((length, 128))
            a_main, _, a_low, a_low_r = fields(alpha_ref, 2 * u, length, at)
            _, b_main_r, b_low, b_low_r = fields(alpha_ref, 2 * u + 1, length, at)
            alphas = (
                a_main,
                jnp.where(left, jnp.concatenate([a_low, a_low_r], 0), b_main_r),
                jnp.where(left, b_main_r, jnp.concatenate([b_low_r, b_low], 0)),
            )
            for n in range(3):
                col = pl.ds(pl.multiple_of(u * 384 + 128 * n, 128), 128)
                out_ref[rows:rows + length, col] = alphas[n] + out_ref[rows:rows + length, col]
        return carry

    copies = []
    for part in range(4):
        lax.fori_loop(4 * part, 4 * part + 4, triple, 0, unroll=2)
        cols = slice(1536 * part, 1536 * part + 1536)
        copy = pltpu.make_async_copy(out_ref.at[:, cols], out_hbm.at[:, cols], out_sems.at[part])
        copy.start()
        copies.append(copy)
    for copy in copies:
        copy.wait()


def in_vmem(x):
    return pltpu.with_memory_space_constraint(x, pltpu.VMEM)


def smem():
    return pl.BlockSpec(memory_space=pltpu.SMEM)


def vmem():
    return pl.BlockSpec(memory_space=pltpu.VMEM)


def hbm():
    return pl.BlockSpec(memory_space=pl.ANY)


def split_table(table):
    tiles = table.reshape(table.shape[0], BLK, BLK)
    hi = lax.reduce_precision(tiles, 8, 7)
    return jnp.concatenate([hi, tiles - hi], 2).astype(bf16)


def on_device(coeffs_t, alpha_table, alpha_blocks, alpha_types, beta_table, beta_blocks, beta_types, row_counts):
    slots = jax.ShapeDtypeStruct((COLS, PACK, 128), f32)
    coeff_slots = pl.pallas_call(
        coeff_kernel,
        in_specs=[smem(), hbm()],
        out_specs=hbm(),
        out_shape=slots,
        scratch_shapes=[
            pltpu.VMEM((LOCAL, NA), f32),
            pltpu.VMEM((COLS, PACK, 128), f32),
            pltpu.VMEM((ROWS, 256), f32),
            pltpu.SemaphoreType.DMA((2,)),
            pltpu.SemaphoreType.DMA((PIECES,)),
        ],
        name="coeff_slots",
    )(row_counts, coeffs_t)
    alpha_slots = pl.pallas_call(
        alpha_kernel,
        in_specs=[smem(), smem(), smem(), vmem(), vmem()],
        out_specs=vmem(),
        out_shape=slots,
        scratch_shapes=[
            pltpu.VMEM((ROWS, 256), f32),
            pltpu.VMEM((NA, 2 * NA), bf16),
            pltpu.VMEM((2 * NA, 256), bf16),
            pltpu.VMEM((2 * NA, 256), bf16),
        ],
        name="alpha_slots",
    )(row_counts, alpha_blocks, alpha_types, coeffs_t, split_table(alpha_table))
    tiles = split_table(beta_table)
    own = lax.all_to_all(coeff_slots, "col", split_axis=0, concat_axis=0, tiled=True)
    own, alpha_slots, tiles = lax.optimization_barrier((own, alpha_slots, tiles))
    route = [(i, i ^ 1) for i in range(8)]
    partner_first = lax.ppermute(own[:, :SPLIT], "cls", route)
    alpha = lax.all_to_all(alpha_slots, "col", split_axis=0, concat_axis=0, tiled=True)
    sizes = [PARTS[0][1], PARTS[1][1]]
    own_first, own_last = pl.pallas_call(
        own_kernel,
        in_specs=[vmem()],
        out_specs=[vmem(), vmem()],
        out_shape=[jax.ShapeDtypeStruct((BLOCKS, size, 256), bf16) for size in sizes],
        name="own_split",
    )(in_vmem(own))
    rest, own_first, own_last = lax.optimization_barrier((own[:, SPLIT:], own_first, own_last))
    partner_last = lax.ppermute(rest, "cls", route)
    blocks, types = beta_blocks.T, beta_types.T
    first = pl.pallas_call(
        first_kernel,
        in_specs=[smem(), smem(), hbm(), vmem(), hbm()],
        out_specs=vmem(),
        out_shape=jax.ShapeDtypeStruct((sizes[0], BLOCKS * BLK), f32),
        scratch_shapes=[
            pltpu.VMEM((2 * BLOCKS, sizes[0], 256), bf16),
            pltpu.VMEM((64, BLK, 128), bf16),
            pltpu.SemaphoreType.DMA((2,)),
        ],
        name="beta_first",
    )(blocks, types, own_first, in_vmem(partner_first), tiles)
    return pl.pallas_call(
        last_kernel,
        in_specs=[smem(), smem(), hbm(), vmem(), hbm(), hbm(), vmem()],
        out_specs=hbm(),
        out_shape=jax.ShapeDtypeStruct((CAP, BLOCKS * BLK), f32),
        scratch_shapes=[
            pltpu.VMEM((2 * BLOCKS, sizes[1], 256), bf16),
            pltpu.VMEM((64, BLK, 128), bf16),
            pltpu.VMEM((CAP, BLOCKS * BLK), f32),
            pltpu.SemaphoreType.DMA((3,)),
            pltpu.SemaphoreType.DMA((4,)),
        ],
        name="beta_last",
    )(blocks, types, own_last, in_vmem(partner_last), tiles, first, in_vmem(alpha))


def solution(mesh):
    return jax.shard_map(
        on_device,
        mesh=mesh,
        in_specs=(P(("cls", "col"), None), P(), P(), P(), P(), P("cls", None), P("cls", None), P()),
        out_specs=P("col", "cls"),
        check_vma=False,
    )
```

```python
import jax
import jax.numpy as jnp
from jax import lax
from jax.experimental import pallas as pl
from jax.experimental.pallas import tpu as pltpu
from jax.sharding import PartitionSpec as P

f32 = jnp.float32
bf16 = jnp.bfloat16

NA = 1024
BLK = 64
COLS = 32
CAP = 48
LOCAL = 192
HALF = CAP // 2
PACK = CAP + HALF
BLOCKS = 96
DEPTH = 12
PARTS = ((0, 32, 0), (32, 16, 48))
SPLIT = 48
TRIP = 24
ROWS = NA + CAP + 8


def split(x):
    hi = x.astype(bf16)
    return hi, (x - hi.astype(f32)).astype(bf16)


def left_half(shape):
    return lax.broadcasted_iota(jnp.int32, shape, len(shape) - 1) < BLK


def transpose_pair(x_ref, buf_ref):
    for c in range(NA // 128):
        cols = slice(128 * c, 128 * c + 128)
        buf_ref[cols, 0:128] = x_ref[0:128, cols].T


def transpose_third(x_ref, buf_ref):
    for c in range(NA // 128):
        cols = slice(128 * c, 128 * c + 128)
        third = x_ref[128:LOCAL, cols]
        buf_ref[cols, 128:256] = jnp.concatenate([third, third], 0).T


def write_slots(counts_ref, buf_ref, out_ref):
    buf_ref[NA:ROWS, :] = jnp.zeros((ROWS - NA, 256), f32)
    left = left_half((8, 128))
    sub = lax.broadcasted_iota(jnp.int32, (8, 256), 0)

    def one(j, start):
        count = counts_ref[j]
        base = pl.multiple_of((start // 8) * 8, 8)
        shift = 8 - (start - base)
        turned = [pltpu.roll(buf_ref[pl.ds(base + 8 * n, 8), :], shift & 7, 0) for n in range(CAP // 8 + 1)]
        main, third = [], []
        for n in range(CAP // 8):
            rows = jnp.where(sub < shift, turned[n], turned[n + 1])
            rows = jnp.where(sub < count - 8 * n, rows, 0.0)
            main.append(rows[:, 0:128])
            third.append(rows[:, 128:256])
        for part in range(2):
            first, size, at = PARTS[part]
            n0, n1 = first // 8, size // 8
            half = n1 // 2
            low = [jnp.where(left, third[n0 + n], third[n0 + half + n]) for n in range(half)]
            out_ref[j, at:at + size, :] = jnp.concatenate(main[n0:n0 + n1], 0)
            out_ref[j, at + size:at + size + size // 2, :] = jnp.concatenate(low, 0) if half > 1 else low[0]
        return start + count

    lax.fori_loop(0, COLS, one, jnp.int32(0))


def coeff_kernel(counts_ref, x_ref, out_ref, buf_ref):
    transpose_pair(x_ref, buf_ref)
    transpose_third(x_ref, buf_ref)
    write_slots(counts_ref, buf_ref, out_ref)


def alpha_kernel(counts_ref, blocks_ref, types_ref, x_ref, table_ref, out_ref, buf_ref, a_ref, hi_ref, lo_ref):
    transpose_pair(x_ref, buf_ref)
    transpose_third(x_ref, buf_ref)
    blocks = NA // BLK
    for b in range(blocks):
        hi, lo = split(buf_ref[BLK * b:BLK * b + BLK, :])
        for half in range(2):
            at = slice(128 * b + BLK * half, 128 * b + BLK * half + BLK)
            hi_ref[at, :] = hi
            lo_ref[at, :] = lo

    def place(i, carry):
        for k in range(blocks):
            col = pl.multiple_of(blocks_ref[i, k] * 128, 128)
            row = pl.multiple_of(i * BLK, BLK)
            a_ref[pl.ds(row, BLK), pl.ds(col, 128)] = table_ref[types_ref[i, k]]
        return carry

    lax.fori_loop(0, blocks, place, 0)
    for r in range(4):
        rows = slice(256 * r, 256 * r + 256)
        a = a_ref[rows, :]
        buf_ref[rows, :] = jnp.dot(a, hi_ref[...], preferred_element_type=f32) + jnp.dot(
            a, lo_ref[...], preferred_element_type=f32
        )
    write_slots(counts_ref, buf_ref, out_ref)


def swap(x):
    return pltpu.roll(x, BLK, 1)


def fields(ref, j, size, at):
    main = ref[j, at:at + size, :]
    low = ref[j, at + size:at + size + size // 2, :]
    return main, swap(main), low, swap(low)


def unpack(ref, size, at, z_ref, base):
    left = left_half((size, 128))
    left_low = left_half((size // 2, 128))

    def one(j, carry):
        main, main_r, low, low_r = fields(ref, j, size, at)
        parts = (
            jnp.where(left, main, main_r),
            jnp.where(left, main_r, main),
            jnp.concatenate([jnp.where(left_low, low, low_r), jnp.where(left_low, low_r, low)], 0),
        )
        for n in range(3):
            hi, lo = split(parts[n])
            z_ref[base + 3 * j + n] = jnp.concatenate([hi, lo], 1)
        return carry

    lax.fori_loop(0, COLS, one, 0, unroll=2)


def own_kernel(own_ref, za_ref, zb_ref):
    for (first, size, at), z_ref in zip(PARTS, (za_ref, zb_ref)):
        unpack(own_ref, size, at, z_ref, 0)


def product(blocks_ref, types_ref, z_ref, table_ref, size, store):
    pick = left_half((size, 256)) | (lax.broadcasted_iota(jnp.int32, (size, 256), 1) // BLK == 2)
    left = left_half((size, 128))

    def block(m):
        hi, lo, w = [], [], []
        for k in range(0, DEPTH, 2):
            pair = jnp.where(pick, z_ref[blocks_ref[k, m]], z_ref[blocks_ref[k + 1, m]])
            hi.append(pair[:, 0:128])
            lo.append(pair[:, 128:256])
            w.append(table_ref[types_ref[k, m]])
            w.append(table_ref[types_ref[k + 1, m]])
        lhs = jnp.concatenate([jnp.concatenate(hi, 1), jnp.concatenate(lo, 1)], 0)
        both = jnp.dot(lhs, jnp.concatenate(w, 0), preferred_element_type=f32)
        both = both[0:size] + both[size:]
        return both + swap(both)

    def trip(n, carry):
        for i in range(TRIP):
            p = n * TRIP + i
            col = pl.ds(pl.multiple_of(p * 128, 128), 128)
            store(col, jnp.where(left, block(2 * p), block(2 * p + 1)))
        return carry

    lax.fori_loop(0, BLOCKS // (2 * TRIP), trip, 0)


def first_kernel(blocks_ref, types_ref, own_hbm, partner_ref, table_hbm, out_ref, z_ref, table_ref, sems):
    size = PARTS[0][1]
    own_copy = pltpu.make_async_copy(own_hbm, z_ref.at[0:BLOCKS], sems.at[0])
    table_copy = pltpu.make_async_copy(table_hbm, table_ref, sems.at[1])
    own_copy.start()
    table_copy.start()
    unpack(partner_ref, size, 0, z_ref, BLOCKS)
    own_copy.wait()
    table_copy.wait()

    def store(col, value):
        out_ref[:, col] = value

    product(blocks_ref, types_ref, z_ref, table_ref, size, store)


def last_kernel(
    blocks_ref, types_ref, own_hbm, partner_ref, table_hbm, first_hbm, alpha_ref, out_hbm,
    z_ref, table_ref, out_ref, sems, out_sems,
):
    (_, size_a, at_a), (start, size, at_b) = PARTS
    own_copy = pltpu.make_async_copy(own_hbm, z_ref.at[0:BLOCKS], sems.at[0])
    first_copy = pltpu.make_async_copy(first_hbm, out_ref.at[0:start, :], sems.at[1])
    table_copy = pltpu.make_async_copy(table_hbm, table_ref, sems.at[2])
    own_copy.start()
    table_copy.start()
    first_copy.start()
    unpack(partner_ref, size, 0, z_ref, BLOCKS)
    own_copy.wait()
    table_copy.wait()

    def store(col, value):
        out_ref[start:CAP, col] = value

    product(blocks_ref, types_ref, z_ref, table_ref, size, store)
    first_copy.wait()

    def triple(u, carry):
        for rows, length, at in ((0, size_a, at_a), (start, size, at_b)):
            left = left_half((length, 128))
            a_main, _, a_low, a_low_r = fields(alpha_ref, 2 * u, length, at)
            _, b_main_r, b_low, b_low_r = fields(alpha_ref, 2 * u + 1, length, at)
            alphas = (
                a_main,
                jnp.where(left, jnp.concatenate([a_low, a_low_r], 0), b_main_r),
                jnp.where(left, b_main_r, jnp.concatenate([b_low_r, b_low], 0)),
            )
            for n in range(3):
                col = pl.ds(pl.multiple_of(u * 384 + 128 * n, 128), 128)
                out_ref[rows:rows + length, col] = alphas[n] + out_ref[rows:rows + length, col]
        return carry

    copies = []
    for part in range(4):
        lax.fori_loop(4 * part, 4 * part + 4, triple, 0, unroll=2)
        cols = slice(1536 * part, 1536 * part + 1536)
        copy = pltpu.make_async_copy(out_ref.at[:, cols], out_hbm.at[:, cols], out_sems.at[part])
        copy.start()
        copies.append(copy)
    for copy in copies:
        copy.wait()


def grant(mib, **kw):
    return pltpu.CompilerParams(vmem_limit_bytes=mib << 20, **kw)


def in_vmem(x):
    return pltpu.with_memory_space_constraint(x, pltpu.VMEM)


def smem():
    return pl.BlockSpec(memory_space=pltpu.SMEM)


def vmem():
    return pl.BlockSpec(memory_space=pltpu.VMEM)


def hbm():
    return pl.BlockSpec(memory_space=pl.ANY)


def split_table(table):
    tiles = table.reshape(table.shape[0], BLK, BLK)
    hi = lax.reduce_precision(tiles, 8, 7)
    return jnp.concatenate([hi, tiles - hi], 2).astype(bf16)


def on_device(coeffs_t, alpha_table, alpha_blocks, alpha_types, beta_table, beta_blocks, beta_types, row_counts):
    slots = jax.ShapeDtypeStruct((COLS, PACK, 128), f32)
    coeff_slots = pl.pallas_call(
        coeff_kernel,
        in_specs=[smem(), vmem()],
        out_specs=vmem(),
        out_shape=slots,
        scratch_shapes=[pltpu.VMEM((ROWS, 256), f32)],
        name="coeff_slots",
    )(row_counts, coeffs_t)
    coeff_slots, alpha_table, beta_table = lax.optimization_barrier((coeff_slots, alpha_table, beta_table))
    alpha_slots = pl.pallas_call(
        alpha_kernel,
        in_specs=[smem(), smem(), smem(), vmem(), vmem()],
        out_specs=vmem(),
        out_shape=slots,
        scratch_shapes=[
            pltpu.VMEM((ROWS, 256), f32),
            pltpu.VMEM((NA, 2 * NA), bf16),
            pltpu.VMEM((2 * NA, 256), bf16),
            pltpu.VMEM((2 * NA, 256), bf16),
        ],
        name="alpha_slots",
    )(row_counts, alpha_blocks, alpha_types, coeffs_t, split_table(alpha_table))
    tiles = split_table(beta_table)
    own = lax.all_to_all(coeff_slots, "col", split_axis=0, concat_axis=0, tiled=True)
    own, alpha_slots, tiles = lax.optimization_barrier((own, alpha_slots, tiles))
    route = [(i, i ^ 1) for i in range(8)]
    partner_first = lax.ppermute(own[:, :SPLIT], "cls", route)
    alpha = lax.all_to_all(alpha_slots, "col", split_axis=0, concat_axis=0, tiled=True)
    sizes = [PARTS[0][1], PARTS[1][1]]
    own_first, own_last = pl.pallas_call(
        own_kernel,
        in_specs=[vmem()],
        out_specs=[vmem(), vmem()],
        out_shape=[jax.ShapeDtypeStruct((BLOCKS, size, 256), bf16) for size in sizes],
        compiler_params=grant(16),
        name="own_split",
    )(in_vmem(own))
    rest, own_first, own_last = lax.optimization_barrier((own[:, SPLIT:], own_first, own_last))
    partner_last = lax.ppermute(rest, "cls", route)
    blocks, types = beta_blocks.T, beta_types.T
    first = pl.pallas_call(
        first_kernel,
        in_specs=[smem(), smem(), hbm(), vmem(), hbm()],
        out_specs=vmem(),
        out_shape=jax.ShapeDtypeStruct((sizes[0], BLOCKS * BLK), f32),
        scratch_shapes=[
            pltpu.VMEM((2 * BLOCKS, sizes[0], 256), bf16),
            pltpu.VMEM((64, BLK, 128), bf16),
            pltpu.SemaphoreType.DMA((2,)),
        ],
        compiler_params=grant(24),
        name="beta_first",
    )(blocks, types, own_first, in_vmem(partner_first), tiles)
    return pl.pallas_call(
        last_kernel,
        in_specs=[smem(), smem(), hbm(), vmem(), hbm(), hbm(), vmem()],
        out_specs=hbm(),
        out_shape=jax.ShapeDtypeStruct((CAP, BLOCKS * BLK), f32),
        scratch_shapes=[
            pltpu.VMEM((2 * BLOCKS, sizes[1], 256), bf16),
            pltpu.VMEM((64, BLK, 128), bf16),
            pltpu.VMEM((CAP, BLOCKS * BLK), f32),
            pltpu.SemaphoreType.DMA((3,)),
            pltpu.SemaphoreType.DMA((4,)),
        ],
        compiler_params=grant(24),
        name="beta_last",
    )(blocks, types, own_last, in_vmem(partner_last), tiles, first, in_vmem(alpha))


def solution(mesh):
    return jax.shard_map(
        on_device,
        mesh=mesh,
        in_specs=(P(("cls", "col"), None), P(), P(), P(), P(), P("cls", None), P("cls", None), P()),
        out_specs=P("col", "cls"),
        check_vma=False,
    )
```

```python
import jax
import jax.numpy as jnp
from jax import lax
from jax.experimental import pallas as pl
from jax.experimental.pallas import tpu as pltpu
from jax.sharding import PartitionSpec as P

f32 = jnp.float32
bf16 = jnp.bfloat16

NA = 1024
BLK = 64
COLS = 32
CAP = 48
LOCAL = 192
HALF = CAP // 2
PACK = CAP + HALF
BLOCKS = 96
DEPTH = 12
PARTS = ((0, 32, 0), (32, 16, 48))
SPLIT = 48
TRIP = 12
ROWS = NA + CAP + 8


def split(x):
    hi = x.astype(bf16)
    return hi, (x - hi.astype(f32)).astype(bf16)


def left_half(shape):
    return lax.broadcasted_iota(jnp.int32, shape, len(shape) - 1) < BLK


def transpose_pair(x_ref, buf_ref):
    for c in range(NA // 128):
        cols = slice(128 * c, 128 * c + 128)
        buf_ref[cols, 0:128] = x_ref[0:128, cols].T


def transpose_third(x_ref, buf_ref):
    for c in range(NA // 128):
        cols = slice(128 * c, 128 * c + 128)
        third = x_ref[128:LOCAL, cols]
        buf_ref[cols, 128:256] = jnp.concatenate([third, third], 0).T


def write_slots(counts_ref, buf_ref, out_ref):
    buf_ref[NA:ROWS, :] = jnp.zeros((ROWS - NA, 256), f32)
    left = left_half((8, 128))
    sub = lax.broadcasted_iota(jnp.int32, (8, 256), 0)

    def one(j, start):
        count = counts_ref[j]
        base = pl.multiple_of((start // 8) * 8, 8)
        shift = 8 - (start - base)
        turned = [pltpu.roll(buf_ref[pl.ds(base + 8 * n, 8), :], shift & 7, 0) for n in range(CAP // 8 + 1)]
        main, third = [], []
        for n in range(CAP // 8):
            rows = jnp.where(sub < shift, turned[n], turned[n + 1])
            rows = jnp.where(sub < count - 8 * n, rows, 0.0)
            main.append(rows[:, 0:128])
            third.append(rows[:, 128:256])
        for part in range(2):
            first, size, at = PARTS[part]
            n0, n1 = first // 8, size // 8
            half = n1 // 2
            low = [jnp.where(left, third[n0 + n], third[n0 + half + n]) for n in range(half)]
            out_ref[j, at:at + size, :] = jnp.concatenate(main[n0:n0 + n1], 0)
            out_ref[j, at + size:at + size + size // 2, :] = jnp.concatenate(low, 0) if half > 1 else low[0]
        return start + count

    lax.fori_loop(0, COLS, one, jnp.int32(0))


def coeff_kernel(counts_ref, x_ref, out_ref, buf_ref):
    transpose_pair(x_ref, buf_ref)
    transpose_third(x_ref, buf_ref)
    write_slots(counts_ref, buf_ref, out_ref)


def alpha_kernel(counts_ref, blocks_ref, types_ref, x_ref, table_ref, out_ref, buf_ref, a_ref, hi_ref, lo_ref):
    transpose_pair(x_ref, buf_ref)
    transpose_third(x_ref, buf_ref)
    blocks = NA // BLK
    for b in range(blocks):
        hi, lo = split(buf_ref[BLK * b:BLK * b + BLK, :])
        for half in range(2):
            at = slice(128 * b + BLK * half, 128 * b + BLK * half + BLK)
            hi_ref[at, :] = hi
            lo_ref[at, :] = lo

    def place(i, carry):
        for k in range(blocks):
            col = pl.multiple_of(blocks_ref[i, k] * 128, 128)
            row = pl.multiple_of(i * BLK, BLK)
            a_ref[pl.ds(row, BLK), pl.ds(col, 128)] = table_ref[types_ref[i, k]]
        return carry

    lax.fori_loop(0, blocks, place, 0)
    for r in range(4):
        rows = slice(256 * r, 256 * r + 256)
        a = a_ref[rows, :]
        buf_ref[rows, :] = jnp.dot(a, hi_ref[...], preferred_element_type=f32) + jnp.dot(
            a, lo_ref[...], preferred_element_type=f32
        )
    write_slots(counts_ref, buf_ref, out_ref)


def swap(x):
    return pltpu.roll(x, BLK, 1)


def fields(ref, j, size, at):
    main = ref[j, at:at + size, :]
    low = ref[j, at + size:at + size + size // 2, :]
    return main, swap(main), low, swap(low)


def unpack(ref, size, at, z_ref, base):
    left = left_half((size, 128))
    left_low = left_half((size // 2, 128))

    def one(j, carry):
        main, main_r, low, low_r = fields(ref, j, size, at)
        parts = (
            jnp.where(left, main, main_r),
            jnp.where(left, main_r, main),
            jnp.concatenate([jnp.where(left_low, low, low_r), jnp.where(left_low, low_r, low)], 0),
        )
        for n in range(3):
            hi, lo = split(parts[n])
            z_ref[base + 3 * j + n] = jnp.concatenate([hi, lo], 1)
        return carry

    lax.fori_loop(0, COLS, one, 0, unroll=2)


def own_kernel(own_ref, za_hbm, zb_hbm, za_ref, zb_ref, sems):
    copies = []
    for n, (z_ref, z_hbm) in enumerate(((za_ref, za_hbm), (zb_ref, zb_hbm))):
        _, size, at = PARTS[n]
        unpack(own_ref, size, at, z_ref, 0)
        copies.append(pltpu.make_async_copy(z_ref, z_hbm, sems.at[n]))
        copies[n].start()
    for copy in copies:
        copy.wait()


def product(blocks_ref, types_ref, z_ref, table_ref, size, trip_pairs, store, before=None, after=None):
    pick = left_half((size, 256)) | (lax.broadcasted_iota(jnp.int32, (size, 256), 1) // BLK == 2)
    left = left_half((size, 128))

    def block(m):
        hi, lo, w = [], [], []
        for k in range(0, DEPTH, 2):
            pair = jnp.where(pick, z_ref[blocks_ref[k, m]], z_ref[blocks_ref[k + 1, m]])
            hi.append(pair[:, 0:128])
            lo.append(pair[:, 128:256])
            w.append(table_ref[types_ref[k, m]])
            w.append(table_ref[types_ref[k + 1, m]])
        lhs = jnp.concatenate([jnp.concatenate(hi, 1), jnp.concatenate(lo, 1)], 0)
        both = jnp.dot(lhs, jnp.concatenate(w, 0), preferred_element_type=f32)
        both = both[0:size] + both[size:]
        return both + swap(both)

    def trip(n, carry):
        for i in range(trip_pairs):
            p = n * trip_pairs + i
            col = pl.ds(pl.multiple_of(p * 128, 128), 128)
            store(p, i % 3, col, jnp.where(left, block(2 * p), block(2 * p + 1)))
        return carry

    if before is None:
        lax.fori_loop(0, BLOCKS // (2 * trip_pairs), trip, 0)
        return
    for n in range(BLOCKS // (2 * trip_pairs)):
        before(n)
        trip(n, 0)
        after(n)


def first_kernel(blocks_ref, types_ref, own_hbm, partner_ref, table_ref, out_ref, z_ref, sem):
    size = PARTS[0][1]
    own_copy = pltpu.make_async_copy(own_hbm, z_ref.at[0:BLOCKS], sem)
    own_copy.start()
    unpack(partner_ref, size, 0, z_ref, BLOCKS)
    own_copy.wait()

    def store(p, kind, col, value):
        out_ref[:, col] = value

    product(blocks_ref, types_ref, z_ref, table_ref, size, 2 * TRIP, store)


def alpha_tile(alpha_ref, u, kind, length, at):
    left = left_half((length, 128))
    if kind == 0:
        return alpha_ref[2 * u, at:at + length, :]
    main = swap(alpha_ref[2 * u + 1, at:at + length, :])
    low_rows = slice(at + length, at + length + length // 2)
    if kind == 1:
        low = alpha_ref[2 * u, low_rows, :]
        return jnp.where(left, jnp.concatenate([low, swap(low)], 0), main)
    low = alpha_ref[2 * u + 1, low_rows, :]
    return jnp.where(left, main, jnp.concatenate([swap(low), low], 0))


def last_kernel(
    blocks_ref, types_ref, own_hbm, partner_ref, table_hbm, first_hbm, alpha_hbm, out_hbm,
    z_ref, table_ref, alpha_ref, out_ref, sems, in_sems, alpha_sems, out_sems,
):
    (_, size_a, at_a), (start, size, at_b) = PARTS
    table_copy = pltpu.make_async_copy(table_hbm, table_ref, sems.at[0])
    own_copy = pltpu.make_async_copy(own_hbm, z_ref.at[0:BLOCKS], sems.at[1])
    table_copy.start()
    own_copy.start()
    pieces = [slice(TRIP * 128 * n, TRIP * 128 * (n + 1)) for n in range(BLOCKS // (2 * TRIP))]
    loads, alphas, stores = [], [], []
    each = COLS // len(pieces)
    for n, cols in enumerate(pieces):
        senders = slice(each * n, each * (n + 1))
        alphas.append(pltpu.make_async_copy(alpha_hbm.at[senders], alpha_ref.at[senders], alpha_sems.at[n]))
        alphas[n].start()
        loads.append(pltpu.make_async_copy(first_hbm.at[:, cols], out_ref.at[0:start, cols], in_sems.at[n]))
        loads[n].start()
    unpack(partner_ref, size, 0, z_ref, BLOCKS)
    table_copy.wait()
    own_copy.wait()

    def store(p, kind, col, value):
        u = p // 3
        out_ref[0:start, col] = alpha_tile(alpha_ref, u, kind, size_a, at_a) + out_ref[0:start, col]
        out_ref[start:CAP, col] = alpha_tile(alpha_ref, u, kind, size, at_b) + value

    def before(n):
        for i in {0: (0,), 1: range(1, len(pieces))}.get(n, ()):
            loads[i].wait()
            alphas[i].wait()

    def after(n):
        stores.append(pltpu.make_async_copy(out_ref.at[:, pieces[n]], out_hbm.at[:, pieces[n]], out_sems.at[n]))
        stores[n].start()

    product(blocks_ref, types_ref, z_ref, table_ref, size, TRIP, store, before, after)
    for copy in stores:
        copy.wait()


def in_vmem(x):
    return pltpu.with_memory_space_constraint(x, pltpu.VMEM)


def smem():
    return pl.BlockSpec(memory_space=pltpu.SMEM)


def vmem():
    return pl.BlockSpec(memory_space=pltpu.VMEM)


def hbm():
    return pl.BlockSpec(memory_space=pl.ANY)


def split_table(table):
    tiles = table.reshape(table.shape[0], BLK, BLK)
    hi = lax.reduce_precision(tiles, 8, 7)
    return jnp.concatenate([hi, tiles - hi], 2).astype(bf16)


def on_device(coeffs_t, alpha_table, alpha_blocks, alpha_types, beta_table, beta_blocks, beta_types, row_counts):
    slots = jax.ShapeDtypeStruct((COLS, PACK, 128), f32)
    coeff_slots = pl.pallas_call(
        coeff_kernel,
        in_specs=[smem(), vmem()],
        out_specs=vmem(),
        out_shape=slots,
        scratch_shapes=[pltpu.VMEM((ROWS, 256), f32)],
        name="coeff_slots",
    )(row_counts, coeffs_t)
    coeff_slots, alpha_table, beta_table = lax.optimization_barrier((coeff_slots, alpha_table, beta_table))
    alpha_slots = pl.pallas_call(
        alpha_kernel,
        in_specs=[smem(), smem(), smem(), vmem(), vmem()],
        out_specs=vmem(),
        out_shape=slots,
        scratch_shapes=[
            pltpu.VMEM((ROWS, 256), f32),
            pltpu.VMEM((NA, 2 * NA), bf16),
            pltpu.VMEM((2 * NA, 256), bf16),
            pltpu.VMEM((2 * NA, 256), bf16),
        ],
        name="alpha_slots",
    )(row_counts, alpha_blocks, alpha_types, coeffs_t, split_table(alpha_table))
    tiles = split_table(beta_table)
    own = lax.all_to_all(coeff_slots, "col", split_axis=0, concat_axis=0, tiled=True)
    own, alpha_slots, tiles = lax.optimization_barrier((own, alpha_slots, tiles))
    route = [(i, i ^ 1) for i in range(8)]
    partner_first = lax.ppermute(own[:, :SPLIT], "cls", route)
    alpha = lax.all_to_all(alpha_slots, "col", split_axis=0, concat_axis=0, tiled=True)
    sizes = [PARTS[0][1], PARTS[1][1]]
    own_first, own_last = pl.pallas_call(
        own_kernel,
        in_specs=[vmem()],
        out_specs=[hbm(), hbm()],
        out_shape=[jax.ShapeDtypeStruct((BLOCKS, size, 256), bf16) for size in sizes],
        scratch_shapes=[pltpu.VMEM((BLOCKS, size, 256), bf16) for size in sizes]
        + [pltpu.SemaphoreType.DMA((2,))],
        name="own_split",
    )(in_vmem(own))
    rest, own_first, own_last = lax.optimization_barrier((own[:, SPLIT:], own_first, own_last))
    partner_last = lax.ppermute(rest, "cls", route)
    blocks, types = beta_blocks.T, beta_types.T
    first = pl.pallas_call(
        first_kernel,
        in_specs=[smem(), smem(), hbm(), vmem(), vmem()],
        out_specs=vmem(),
        out_shape=jax.ShapeDtypeStruct((sizes[0], BLOCKS * BLK), f32),
        scratch_shapes=[
            pltpu.VMEM((2 * BLOCKS, sizes[0], 256), bf16),
            pltpu.SemaphoreType.DMA,
        ],
        name="beta_first",
    )(blocks, types, own_first, in_vmem(partner_first), in_vmem(tiles))
    return pl.pallas_call(
        last_kernel,
        in_specs=[smem(), smem(), hbm(), vmem(), hbm(), hbm(), hbm()],
        out_specs=hbm(),
        out_shape=jax.ShapeDtypeStruct((CAP, BLOCKS * BLK), f32),
        scratch_shapes=[
            pltpu.VMEM((2 * BLOCKS, sizes[1], 256), bf16),
            pltpu.VMEM((64, BLK, 128), bf16),
            pltpu.VMEM((COLS, PACK, 128), f32),
            pltpu.VMEM((CAP, BLOCKS * BLK), f32),
            pltpu.SemaphoreType.DMA((2,)),
            pltpu.SemaphoreType.DMA((BLOCKS // (2 * TRIP),)),
            pltpu.SemaphoreType.DMA((BLOCKS // (2 * TRIP),)),
            pltpu.SemaphoreType.DMA((BLOCKS // (2 * TRIP),)),
        ],
        name="beta_last",
    )(blocks, types, own_last, in_vmem(partner_last), tiles, first, alpha)


def solution(mesh):
    return jax.shard_map(
        on_device,
        mesh=mesh,
        in_specs=(P(("cls", "col"), None), P(), P(), P(), P(), P("cls", None), P("cls", None), P()),
        out_specs=P("col", "cls"),
        check_vma=False,
    )
```

```python
import jax
import jax.numpy as jnp
from jax import lax
from jax.experimental import pallas as pl
from jax.experimental.pallas import tpu as pltpu
from jax.sharding import PartitionSpec as P

f32 = jnp.float32
bf16 = jnp.bfloat16

NA = 1024
BLK = 64
COLS = 32
CAP = 48
LOCAL = 192
HALF = CAP // 2
PACK = CAP + HALF
BLOCKS = 96
DEPTH = 12
PARTS = ((0, 32, 0), (32, 16, 48))
SPLIT = 48
TRIP = 12
ROWS = NA + CAP + 8


def split(x):
    hi = x.astype(bf16)
    return hi, (x - hi.astype(f32)).astype(bf16)


def left_half(shape):
    return lax.broadcasted_iota(jnp.int32, shape, len(shape) - 1) < BLK


def transpose_pair(x_ref, buf_ref):
    for c in range(NA // 128):
        cols = slice(128 * c, 128 * c + 128)
        buf_ref[cols, 0:128] = x_ref[0:128, cols].T


def transpose_third(x_ref, buf_ref):
    for c in range(NA // 128):
        cols = slice(128 * c, 128 * c + 128)
        third = x_ref[128:LOCAL, cols]
        buf_ref[cols, 128:256] = jnp.concatenate([third, third], 0).T


def write_slots(counts_ref, buf_ref, out_ref):
    buf_ref[NA:ROWS, :] = jnp.zeros((ROWS - NA, 256), f32)
    left = left_half((8, 128))
    sub = lax.broadcasted_iota(jnp.int32, (8, 256), 0)

    def one(j, start):
        count = counts_ref[j]
        base = pl.multiple_of((start // 8) * 8, 8)
        shift = 8 - (start - base)
        turned = [pltpu.roll(buf_ref[pl.ds(base + 8 * n, 8), :], shift & 7, 0) for n in range(CAP // 8 + 1)]
        main, third = [], []
        for n in range(CAP // 8):
            rows = jnp.where(sub < shift, turned[n], turned[n + 1])
            rows = jnp.where(sub < count - 8 * n, rows, 0.0)
            main.append(rows[:, 0:128])
            third.append(rows[:, 128:256])
        for part in range(2):
            first, size, at = PARTS[part]
            n0, n1 = first // 8, size // 8
            half = n1 // 2
            low = [jnp.where(left, third[n0 + n], third[n0 + half + n]) for n in range(half)]
            out_ref[j, at:at + size, :] = jnp.concatenate(main[n0:n0 + n1], 0)
            out_ref[j, at + size:at + size + size // 2, :] = jnp.concatenate(low, 0) if half > 1 else low[0]
        return start + count

    lax.fori_loop(0, COLS, one, jnp.int32(0))


def coeff_kernel(counts_ref, x_ref, out_ref, buf_ref):
    transpose_pair(x_ref, buf_ref)
    transpose_third(x_ref, buf_ref)
    write_slots(counts_ref, buf_ref, out_ref)


def alpha_kernel(counts_ref, blocks_ref, types_ref, x_ref, table_ref, out_ref, buf_ref, a_ref, hi_ref, lo_ref):
    transpose_pair(x_ref, buf_ref)
    transpose_third(x_ref, buf_ref)
    blocks = NA // BLK
    for b in range(blocks):
        hi, lo = split(buf_ref[BLK * b:BLK * b + BLK, :])
        for half in range(2):
            at = slice(128 * b + BLK * half, 128 * b + BLK * half + BLK)
            hi_ref[at, :] = hi
            lo_ref[at, :] = lo

    def place(i, carry):
        for k in range(blocks):
            col = pl.multiple_of(blocks_ref[i, k] * 128, 128)
            row = pl.multiple_of(i * BLK, BLK)
            a_ref[pl.ds(row, BLK), pl.ds(col, 128)] = table_ref[types_ref[i, k]]
        return carry

    lax.fori_loop(0, blocks, place, 0)
    for r in range(4):
        rows = slice(256 * r, 256 * r + 256)
        a = a_ref[rows, :]
        buf_ref[rows, :] = jnp.dot(a, hi_ref[...], preferred_element_type=f32) + jnp.dot(
            a, lo_ref[...], preferred_element_type=f32
        )
    write_slots(counts_ref, buf_ref, out_ref)


def swap(x):
    return pltpu.roll(x, BLK, 1)


def fields(ref, j, size, at):
    main = ref[j, at:at + size, :]
    low = ref[j, at + size:at + size + size // 2, :]
    return main, swap(main), low, swap(low)


def unpack(ref, size, at, z_ref, base):
    left = left_half((size, 128))
    left_low = left_half((size // 2, 128))

    def one(j, carry):
        main, main_r, low, low_r = fields(ref, j, size, at)
        parts = (
            jnp.where(left, main, main_r),
            jnp.where(left, main_r, main),
            jnp.concatenate([jnp.where(left_low, low, low_r), jnp.where(left_low, low_r, low)], 0),
        )
        for n in range(3):
            hi, lo = split(parts[n])
            z_ref[base + 3 * j + n] = jnp.concatenate([hi, lo], 1)
        return carry

    lax.fori_loop(0, COLS, one, 0, unroll=2)


def own_kernel(own_ref, za_hbm, zb_hbm, za_ref, zb_ref, sems):
    copies = []
    for n, (z_ref, z_hbm) in enumerate(((za_ref, za_hbm), (zb_ref, zb_hbm))):
        _, size, at = PARTS[n]
        unpack(own_ref, size, at, z_ref, 0)
        copies.append(pltpu.make_async_copy(z_ref, z_hbm, sems.at[n]))
        copies[n].start()
    for copy in copies:
        copy.wait()


def product(blocks_ref, types_ref, z_ref, table_ref, size, trip_pairs, store, before=None, after=None):
    pick = left_half((size, 256)) | (lax.broadcasted_iota(jnp.int32, (size, 256), 1) // BLK == 2)
    left = left_half((size, 128))

    def block(m):
        hi, lo, w = [], [], []
        for k in range(0, DEPTH, 2):
            pair = jnp.where(pick, z_ref[blocks_ref[k, m]], z_ref[blocks_ref[k + 1, m]])
            hi.append(pair[:, 0:128])
            lo.append(pair[:, 128:256])
            w.append(table_ref[types_ref[k, m]])
            w.append(table_ref[types_ref[k + 1, m]])
        lhs = jnp.concatenate([jnp.concatenate(hi, 1), jnp.concatenate(lo, 1)], 0)
        both = jnp.dot(lhs, jnp.concatenate(w, 0), preferred_element_type=f32)
        both = both[0:size] + both[size:]
        return both + swap(both)

    def trip(n, carry):
        for i in range(trip_pairs):
            p = n * trip_pairs + i
            col = pl.ds(pl.multiple_of(p * 128, 128), 128)
            store(p, i % 3, col, jnp.where(left, block(2 * p), block(2 * p + 1)))
        return carry

    if before is None:
        lax.fori_loop(0, BLOCKS // (2 * trip_pairs), trip, 0)
        return
    for n in range(BLOCKS // (2 * trip_pairs)):
        before(n)
        trip(n, 0)
        after(n)


def first_kernel(blocks_ref, types_ref, own_hbm, partner_hbm, table_hbm, out_ref, z_ref, partner_ref, table_ref, sems):
    size = PARTS[0][1]
    partner_copy = pltpu.make_async_copy(partner_hbm, partner_ref, sems.at[0])
    own_copy = pltpu.make_async_copy(own_hbm, z_ref.at[0:BLOCKS], sems.at[1])
    table_copy = pltpu.make_async_copy(table_hbm, table_ref, sems.at[2])
    partner_copy.start()
    own_copy.start()
    table_copy.start()
    partner_copy.wait()
    unpack(partner_ref, size, 0, z_ref, BLOCKS)
    own_copy.wait()
    table_copy.wait()

    def store(p, kind, col, value):
        out_ref[:, col] = value

    product(blocks_ref, types_ref, z_ref, table_ref, size, 2 * TRIP, store)


def alpha_tile(alpha_ref, u, kind, length, at):
    left = left_half((length, 128))
    if kind == 0:
        return alpha_ref[2 * u, at:at + length, :]
    main = swap(alpha_ref[2 * u + 1, at:at + length, :])
    low_rows = slice(at + length, at + length + length // 2)
    if kind == 1:
        low = alpha_ref[2 * u, low_rows, :]
        return jnp.where(left, jnp.concatenate([low, swap(low)], 0), main)
    low = alpha_ref[2 * u + 1, low_rows, :]
    return jnp.where(left, main, jnp.concatenate([swap(low), low], 0))


def last_kernel(
    blocks_ref, types_ref, own_hbm, partner_ref, table_hbm, first_hbm, alpha_hbm, out_hbm,
    z_ref, table_ref, alpha_ref, out_ref, sems, in_sems, alpha_sems, out_sems,
):
    (_, size_a, at_a), (start, size, at_b) = PARTS
    table_copy = pltpu.make_async_copy(table_hbm, table_ref, sems.at[0])
    own_copy = pltpu.make_async_copy(own_hbm, z_ref.at[0:BLOCKS], sems.at[1])
    table_copy.start()
    own_copy.start()
    pieces = [slice(TRIP * 128 * n, TRIP * 128 * (n + 1)) for n in range(BLOCKS // (2 * TRIP))]
    loads, alphas, stores = [], [], []
    each = COLS // len(pieces)
    for n, cols in enumerate(pieces):
        senders = slice(each * n, each * (n + 1))
        alphas.append(pltpu.make_async_copy(alpha_hbm.at[senders], alpha_ref.at[senders], alpha_sems.at[n]))
        alphas[n].start()
        loads.append(pltpu.make_async_copy(first_hbm.at[:, cols], out_ref.at[0:start, cols], in_sems.at[n]))
        loads[n].start()
    unpack(partner_ref, size, 0, z_ref, BLOCKS)
    table_copy.wait()
    own_copy.wait()

    def store(p, kind, col, value):
        u = p // 3
        out_ref[0:start, col] = alpha_tile(alpha_ref, u, kind, size_a, at_a) + out_ref[0:start, col]
        out_ref[start:CAP, col] = alpha_tile(alpha_ref, u, kind, size, at_b) + value

    def before(n):
        for i in {0: (0,), 1: range(1, len(pieces))}.get(n, ()):
            loads[i].wait()
            alphas[i].wait()

    def after(n):
        stores.append(pltpu.make_async_copy(out_ref.at[:, pieces[n]], out_hbm.at[:, pieces[n]], out_sems.at[n]))
        stores[n].start()

    product(blocks_ref, types_ref, z_ref, table_ref, size, TRIP, store, before, after)
    for copy in stores:
        copy.wait()


def in_vmem(x):
    return pltpu.with_memory_space_constraint(x, pltpu.VMEM)


def smem():
    return pl.BlockSpec(memory_space=pltpu.SMEM)


def vmem():
    return pl.BlockSpec(memory_space=pltpu.VMEM)


def hbm():
    return pl.BlockSpec(memory_space=pl.ANY)


def split_table(table):
    tiles = table.reshape(table.shape[0], BLK, BLK)
    hi = lax.reduce_precision(tiles, 8, 7)
    return jnp.concatenate([hi, tiles - hi], 2).astype(bf16)


def on_device(coeffs_t, alpha_table, alpha_blocks, alpha_types, beta_table, beta_blocks, beta_types, row_counts):
    slots = jax.ShapeDtypeStruct((COLS, PACK, 128), f32)
    coeff_slots = pl.pallas_call(
        coeff_kernel,
        in_specs=[smem(), vmem()],
        out_specs=vmem(),
        out_shape=slots,
        scratch_shapes=[pltpu.VMEM((ROWS, 256), f32)],
        name="coeff_slots",
    )(row_counts, coeffs_t)
    coeff_slots, alpha_table, beta_table = lax.optimization_barrier((coeff_slots, alpha_table, beta_table))
    alpha_slots = pl.pallas_call(
        alpha_kernel,
        in_specs=[smem(), smem(), smem(), vmem(), vmem()],
        out_specs=vmem(),
        out_shape=slots,
        scratch_shapes=[
            pltpu.VMEM((ROWS, 256), f32),
            pltpu.VMEM((NA, 2 * NA), bf16),
            pltpu.VMEM((2 * NA, 256), bf16),
            pltpu.VMEM((2 * NA, 256), bf16),
        ],
        name="alpha_slots",
    )(row_counts, alpha_blocks, alpha_types, coeffs_t, split_table(alpha_table))
    own = lax.all_to_all(coeff_slots, "col", split_axis=0, concat_axis=0, tiled=True)
    own, alpha_slots = lax.optimization_barrier((own, alpha_slots))
    route = [(i, i ^ 1) for i in range(8)]
    partner_first = lax.ppermute(own[:, :SPLIT], "cls", route)
    alpha = lax.all_to_all(alpha_slots, "col", split_axis=0, concat_axis=0, tiled=True)
    sizes = [PARTS[0][1], PARTS[1][1]]
    own_first, own_last = pl.pallas_call(
        own_kernel,
        in_specs=[vmem()],
        out_specs=[hbm(), hbm()],
        out_shape=[jax.ShapeDtypeStruct((BLOCKS, size, 256), bf16) for size in sizes],
        scratch_shapes=[pltpu.VMEM((BLOCKS, size, 256), bf16) for size in sizes]
        + [pltpu.SemaphoreType.DMA((2,))],
        name="own_split",
    )(in_vmem(own))
    rest, own_first, own_last, beta_table = lax.optimization_barrier(
        (own[:, SPLIT:], own_first, own_last, beta_table)
    )
    tiles = split_table(beta_table)
    partner_last = lax.ppermute(rest, "cls", route)
    blocks, types = beta_blocks.T, beta_types.T
    first = pl.pallas_call(
        first_kernel,
        in_specs=[smem(), smem(), hbm(), hbm(), hbm()],
        out_specs=vmem(),
        out_shape=jax.ShapeDtypeStruct((sizes[0], BLOCKS * BLK), f32),
        scratch_shapes=[
            pltpu.VMEM((2 * BLOCKS, sizes[0], 256), bf16),
            pltpu.VMEM((COLS, SPLIT, 128), f32),
            pltpu.VMEM((64, BLK, 128), bf16),
            pltpu.SemaphoreType.DMA((3,)),
        ],
        name="beta_first",
    )(blocks, types, own_first, partner_first, tiles)
    return pl.pallas_call(
        last_kernel,
        in_specs=[smem(), smem(), hbm(), vmem(), hbm(), hbm(), hbm()],
        out_specs=hbm(),
        out_shape=jax.ShapeDtypeStruct((CAP, BLOCKS * BLK), f32),
        scratch_shapes=[
            pltpu.VMEM((2 * BLOCKS, sizes[1], 256), bf16),
            pltpu.VMEM((64, BLK, 128), bf16),
            pltpu.VMEM((COLS, PACK, 128), f32),
            pltpu.VMEM((CAP, BLOCKS * BLK), f32),
            pltpu.SemaphoreType.DMA((2,)),
            pltpu.SemaphoreType.DMA((BLOCKS // (2 * TRIP),)),
            pltpu.SemaphoreType.DMA((BLOCKS // (2 * TRIP),)),
            pltpu.SemaphoreType.DMA((BLOCKS // (2 * TRIP),)),
        ],
        name="beta_last",
    )(blocks, types, own_last, in_vmem(partner_last), tiles, first, alpha)


def solution(mesh):
    return jax.shard_map(
        on_device,
        mesh=mesh,
        in_specs=(P(("cls", "col"), None), P(), P(), P(), P(), P("cls", None), P("cls", None), P()),
        out_specs=P("col", "cls"),
        check_vma=False,
    )
```

```python
import jax
import jax.numpy as jnp
from jax import lax
from jax.experimental import pallas as pl
from jax.experimental.pallas import tpu as pltpu
from jax.sharding import PartitionSpec as P

f32 = jnp.float32
bf16 = jnp.bfloat16

NA = 1024
BLK = 64
COLS = 32
CAP = 48
LOCAL = 192
HALF = CAP // 2
PACK = CAP + HALF
BLOCKS = 96
DEPTH = 12
PARTS = ((0, 32, 0), (32, 16, 48))
SPLIT = 48
TRIP = 12
ROWS = NA + CAP + 8


def split(x):
    hi = x.astype(bf16)
    return hi, (x - hi.astype(f32)).astype(bf16)


def left_half(shape):
    return lax.broadcasted_iota(jnp.int32, shape, len(shape) - 1) < BLK


def transpose_pair(x_ref, buf_ref):
    for c in range(NA // 128):
        cols = slice(128 * c, 128 * c + 128)
        buf_ref[cols, 0:128] = x_ref[0:128, cols].T


def transpose_third(x_ref, buf_ref):
    for c in range(NA // 128):
        cols = slice(128 * c, 128 * c + 128)
        third = x_ref[128:LOCAL, cols]
        buf_ref[cols, 128:256] = jnp.concatenate([third, third], 0).T


def write_slots(counts_ref, buf_ref, out_ref):
    buf_ref[NA:ROWS, :] = jnp.zeros((ROWS - NA, 256), f32)
    left = left_half((8, 128))
    sub = lax.broadcasted_iota(jnp.int32, (8, 256), 0)

    def one(j, start):
        count = counts_ref[j]
        base = pl.multiple_of((start // 8) * 8, 8)
        shift = 8 - (start - base)
        turned = [pltpu.roll(buf_ref[pl.ds(base + 8 * n, 8), :], shift & 7, 0) for n in range(CAP // 8 + 1)]
        main, third = [], []
        for n in range(CAP // 8):
            rows = jnp.where(sub < shift, turned[n], turned[n + 1])
            rows = jnp.where(sub < count - 8 * n, rows, 0.0)
            main.append(rows[:, 0:128])
            third.append(rows[:, 128:256])
        for part in range(2):
            first, size, at = PARTS[part]
            n0, n1 = first // 8, size // 8
            half = n1 // 2
            low = [jnp.where(left, third[n0 + n], third[n0 + half + n]) for n in range(half)]
            out_ref[j, at:at + size, :] = jnp.concatenate(main[n0:n0 + n1], 0)
            out_ref[j, at + size:at + size + size // 2, :] = jnp.concatenate(low, 0) if half > 1 else low[0]
        return start + count

    lax.fori_loop(0, COLS, one, jnp.int32(0))


def coeff_kernel(counts_ref, x_ref, out_ref, buf_ref):
    transpose_pair(x_ref, buf_ref)
    transpose_third(x_ref, buf_ref)
    write_slots(counts_ref, buf_ref, out_ref)


def alpha_kernel(counts_ref, blocks_ref, types_ref, x_ref, table_ref, out_ref, buf_ref, a_ref, hi_ref, lo_ref):
    transpose_pair(x_ref, buf_ref)
    transpose_third(x_ref, buf_ref)
    blocks = NA // BLK
    for b in range(blocks):
        hi, lo = split(buf_ref[BLK * b:BLK * b + BLK, :])
        for half in range(2):
            at = slice(128 * b + BLK * half, 128 * b + BLK * half + BLK)
            hi_ref[at, :] = hi
            lo_ref[at, :] = lo

    def place(i, carry):
        for k in range(blocks):
            col = pl.multiple_of(blocks_ref[i, k] * 128, 128)
            row = pl.multiple_of(i * BLK, BLK)
            a_ref[pl.ds(row, BLK), pl.ds(col, 128)] = table_ref[types_ref[i, k]]
        return carry

    lax.fori_loop(0, blocks, place, 0)
    for r in range(4):
        rows = slice(256 * r, 256 * r + 256)
        a = a_ref[rows, :]
        buf_ref[rows, :] = jnp.dot(a, hi_ref[...], preferred_element_type=f32) + jnp.dot(
            a, lo_ref[...], preferred_element_type=f32
        )
    write_slots(counts_ref, buf_ref, out_ref)


def swap(x):
    return pltpu.roll(x, BLK, 1)


def fields(ref, j, size, at):
    main = ref[j, at:at + size, :]
    low = ref[j, at + size:at + size + size // 2, :]
    return main, swap(main), low, swap(low)


def unpack(ref, size, at, z_ref, base):
    left = left_half((size, 128))
    left_low = left_half((size // 2, 128))

    def one(j, carry):
        main, main_r, low, low_r = fields(ref, j, size, at)
        parts = (
            jnp.where(left, main, main_r),
            jnp.where(left, main_r, main),
            jnp.concatenate([jnp.where(left_low, low, low_r), jnp.where(left_low, low_r, low)], 0),
        )
        for n in range(3):
            hi, lo = split(parts[n])
            z_ref[base + 3 * j + n] = jnp.concatenate([hi, lo], 1)
        return carry

    lax.fori_loop(0, COLS, one, 0, unroll=2)


def own_kernel(own_ref, za_hbm, zb_hbm, za_ref, zb_ref, sems):
    copies = []
    for n, (z_ref, z_hbm) in enumerate(((za_ref, za_hbm), (zb_ref, zb_hbm))):
        _, size, at = PARTS[n]
        unpack(own_ref, size, at, z_ref, 0)
        copies.append(pltpu.make_async_copy(z_ref, z_hbm, sems.at[n]))
        copies[n].start()
    for copy in copies:
        copy.wait()


def product(blocks_ref, types_ref, z_ref, table_ref, size, trip_pairs, store, before=None, after=None):
    pick = left_half((size, 256)) | (lax.broadcasted_iota(jnp.int32, (size, 256), 1) // BLK == 2)
    left = left_half((size, 128))

    def block(m):
        hi, lo, w = [], [], []
        for k in range(0, DEPTH, 2):
            pair = jnp.where(pick, z_ref[blocks_ref[k, m]], z_ref[blocks_ref[k + 1, m]])
            hi.append(pair[:, 0:128])
            lo.append(pair[:, 128:256])
            w.append(table_ref[types_ref[k, m]])
            w.append(table_ref[types_ref[k + 1, m]])
        lhs = jnp.concatenate([jnp.concatenate(hi, 1), jnp.concatenate(lo, 1)], 0)
        both = jnp.dot(lhs, jnp.concatenate(w, 0), preferred_element_type=f32)
        both = both[0:size] + both[size:]
        return both + swap(both)

    def trip(n, carry):
        for i in range(trip_pairs):
            p = n * trip_pairs + i
            col = pl.ds(pl.multiple_of(p * 128, 128), 128)
            store(p, i % 3, col, jnp.where(left, block(2 * p), block(2 * p + 1)))
        return carry

    if before is None:
        lax.fori_loop(0, BLOCKS // (2 * trip_pairs), trip, 0)
        return
    for n in range(BLOCKS // (2 * trip_pairs)):
        before(n)
        trip(n, 0)
        after(n)


def first_kernel(blocks_ref, types_ref, own_hbm, partner_ref, table_ref, out_ref, z_ref, sem):
    size = PARTS[0][1]
    own_copy = pltpu.make_async_copy(own_hbm, z_ref.at[0:BLOCKS], sem)
    own_copy.start()
    unpack(partner_ref, size, 0, z_ref, BLOCKS)
    own_copy.wait()

    def store(p, kind, col, value):
        out_ref[:, col] = value

    product(blocks_ref, types_ref, z_ref, table_ref, size, 2 * TRIP, store)


def alpha_tile(alpha_ref, u, kind, length, at):
    left = left_half((length, 128))
    if kind == 0:
        return alpha_ref[2 * u, at:at + length, :]
    main = swap(alpha_ref[2 * u + 1, at:at + length, :])
    low_rows = slice(at + length, at + length + length // 2)
    if kind == 1:
        low = alpha_ref[2 * u, low_rows, :]
        return jnp.where(left, jnp.concatenate([low, swap(low)], 0), main)
    low = alpha_ref[2 * u + 1, low_rows, :]
    return jnp.where(left, main, jnp.concatenate([swap(low), low], 0))


def last_kernel(
    blocks_ref, types_ref, own_ref, partner_ref, table_ref, first_hbm, alpha_hbm, out_hbm,
    z_ref, alpha_ref, out_ref, sem, in_sems, alpha_sems, out_sems,
):
    (_, size_a, at_a), (start, size, at_b) = PARTS
    own_copy = pltpu.make_async_copy(own_ref, z_ref.at[0:BLOCKS], sem)
    own_copy.start()
    pieces = [slice(TRIP * 128 * n, TRIP * 128 * (n + 1)) for n in range(BLOCKS // (2 * TRIP))]
    loads, alphas, stores = [], [], []
    each = COLS // len(pieces)
    for n, cols in enumerate(pieces):
        senders = slice(each * n, each * (n + 1))
        alphas.append(pltpu.make_async_copy(alpha_hbm.at[senders], alpha_ref.at[senders], alpha_sems.at[n]))
        alphas[n].start()
        loads.append(pltpu.make_async_copy(first_hbm.at[:, cols], out_ref.at[0:start, cols], in_sems.at[n]))
        loads[n].start()
    unpack(partner_ref, size, 0, z_ref, BLOCKS)
    own_copy.wait()

    def store(p, kind, col, value):
        u = p // 3
        out_ref[0:start, col] = alpha_tile(alpha_ref, u, kind, size_a, at_a) + out_ref[0:start, col]
        out_ref[start:CAP, col] = alpha_tile(alpha_ref, u, kind, size, at_b) + value

    def before(n):
        for i in {0: (0,), 1: range(1, len(pieces))}.get(n, ()):
            loads[i].wait()
            alphas[i].wait()

    def after(n):
        stores.append(pltpu.make_async_copy(out_ref.at[:, pieces[n]], out_hbm.at[:, pieces[n]], out_sems.at[n]))
        stores[n].start()

    product(blocks_ref, types_ref, z_ref, table_ref, size, TRIP, store, before, after)
    for copy in stores:
        copy.wait()


def grant(mib, **kw):
    return pltpu.CompilerParams(vmem_limit_bytes=mib << 20, **kw)


def in_vmem(x):
    return pltpu.with_memory_space_constraint(x, pltpu.VMEM)


def smem():
    return pl.BlockSpec(memory_space=pltpu.SMEM)


def vmem():
    return pl.BlockSpec(memory_space=pltpu.VMEM)


def hbm():
    return pl.BlockSpec(memory_space=pl.ANY)


def split_table(table):
    tiles = table.reshape(table.shape[0], BLK, BLK)
    hi = lax.reduce_precision(tiles, 8, 7)
    return jnp.concatenate([hi, tiles - hi], 2).astype(bf16)


def on_device(coeffs_t, alpha_table, alpha_blocks, alpha_types, beta_table, beta_blocks, beta_types, row_counts):
    slots = jax.ShapeDtypeStruct((COLS, PACK, 128), f32)
    coeff_slots = pl.pallas_call(
        coeff_kernel,
        in_specs=[smem(), vmem()],
        out_specs=vmem(),
        out_shape=slots,
        scratch_shapes=[pltpu.VMEM((ROWS, 256), f32)],
        name="coeff_slots",
    )(row_counts, coeffs_t)
    coeff_slots, alpha_table, beta_table = lax.optimization_barrier((coeff_slots, alpha_table, beta_table))
    alpha_slots = pl.pallas_call(
        alpha_kernel,
        in_specs=[smem(), smem(), smem(), vmem(), vmem()],
        out_specs=vmem(),
        out_shape=slots,
        scratch_shapes=[
            pltpu.VMEM((ROWS, 256), f32),
            pltpu.VMEM((NA, 2 * NA), bf16),
            pltpu.VMEM((2 * NA, 256), bf16),
            pltpu.VMEM((2 * NA, 256), bf16),
        ],
        name="alpha_slots",
    )(row_counts, alpha_blocks, alpha_types, coeffs_t, split_table(alpha_table))
    own = lax.all_to_all(coeff_slots, "col", split_axis=0, concat_axis=0, tiled=True)
    own, alpha_slots = lax.optimization_barrier((own, alpha_slots))
    route = [(i, i ^ 1) for i in range(8)]
    partner_first = lax.ppermute(own[:, :SPLIT], "cls", route)
    alpha = lax.all_to_all(alpha_slots, "col", split_axis=0, concat_axis=0, tiled=True)
    sizes = [PARTS[0][1], PARTS[1][1]]
    own_first, own_last = pl.pallas_call(
        own_kernel,
        in_specs=[vmem()],
        out_specs=[hbm(), hbm()],
        out_shape=[jax.ShapeDtypeStruct((BLOCKS, size, 256), bf16) for size in sizes],
        scratch_shapes=[pltpu.VMEM((BLOCKS, size, 256), bf16) for size in sizes]
        + [pltpu.SemaphoreType.DMA((2,))],
        name="own_split",
    )(in_vmem(own))
    rest, own_first, own_last, beta_table = lax.optimization_barrier(
        (own[:, SPLIT:], own_first, own_last, beta_table)
    )
    tiles = split_table(beta_table)
    partner_last = lax.ppermute(rest, "cls", route)
    blocks, types = beta_blocks.T, beta_types.T
    first = pl.pallas_call(
        first_kernel,
        in_specs=[smem(), smem(), hbm(), vmem(), vmem()],
        out_specs=vmem(),
        out_shape=jax.ShapeDtypeStruct((sizes[0], BLOCKS * BLK), f32),
        scratch_shapes=[
            pltpu.VMEM((2 * BLOCKS, sizes[0], 256), bf16),
            pltpu.SemaphoreType.DMA,
        ],
        compiler_params=grant(24),
        name="beta_first",
    )(blocks, types, own_first, in_vmem(partner_first), in_vmem(tiles))
    return pl.pallas_call(
        last_kernel,
        in_specs=[smem(), smem(), vmem(), vmem(), vmem(), hbm(), hbm()],
        out_specs=hbm(),
        out_shape=jax.ShapeDtypeStruct((CAP, BLOCKS * BLK), f32),
        scratch_shapes=[
            pltpu.VMEM((2 * BLOCKS, sizes[1], 256), bf16),
            pltpu.VMEM((COLS, PACK, 128), f32),
            pltpu.VMEM((CAP, BLOCKS * BLK), f32),
            pltpu.SemaphoreType.DMA,
            pltpu.SemaphoreType.DMA((BLOCKS // (2 * TRIP),)),
            pltpu.SemaphoreType.DMA((BLOCKS // (2 * TRIP),)),
            pltpu.SemaphoreType.DMA((BLOCKS // (2 * TRIP),)),
        ],
        name="beta_last",
    )(blocks, types, in_vmem(own_last), in_vmem(partner_last), in_vmem(tiles), first, alpha)


def solution(mesh):
    return jax.shard_map(
        on_device,
        mesh=mesh,
        in_specs=(P(("cls", "col"), None), P(), P(), P(), P(), P("cls", None), P("cls", None), P()),
        out_specs=P("col", "cls"),
        check_vma=False,
    )
```

```python
import jax
import jax.numpy as jnp
from jax import lax
from jax.experimental import pallas as pl
from jax.experimental.pallas import tpu as pltpu
from jax.sharding import PartitionSpec as P

f32 = jnp.float32
bf16 = jnp.bfloat16

NA = 1024
BLK = 64
COLS = 32
CAP = 48
LOCAL = 192
HALF = CAP // 2
PACK = CAP + HALF
BLOCKS = 96
DEPTH = 12
PARTS = ((0, 32, 0), (32, 16, 48))
SPLIT = 48
TRIP = 6
ROWS = NA + CAP + 8


def split(x):
    hi = x.astype(bf16)
    return hi, (x - hi.astype(f32)).astype(bf16)


def left_half(shape):
    return lax.broadcasted_iota(jnp.int32, shape, len(shape) - 1) < BLK


def transpose_pair(x_ref, buf_ref):
    for c in range(NA // 128):
        cols = slice(128 * c, 128 * c + 128)
        buf_ref[cols, 0:128] = x_ref[0:128, cols].T


def transpose_third(x_ref, buf_ref):
    for c in range(NA // 128):
        cols = slice(128 * c, 128 * c + 128)
        third = x_ref[128:LOCAL, cols]
        buf_ref[cols, 128:256] = jnp.concatenate([third, third], 0).T


def write_slots(counts_ref, buf_ref, out_ref):
    buf_ref[NA:ROWS, :] = jnp.zeros((ROWS - NA, 256), f32)
    left = left_half((8, 128))
    sub = lax.broadcasted_iota(jnp.int32, (8, 256), 0)

    def one(j, start):
        count = counts_ref[j]
        base = pl.multiple_of((start // 8) * 8, 8)
        shift = 8 - (start - base)
        turned = [pltpu.roll(buf_ref[pl.ds(base + 8 * n, 8), :], shift & 7, 0) for n in range(CAP // 8 + 1)]
        main, third = [], []
        for n in range(CAP // 8):
            rows = jnp.where(sub < shift, turned[n], turned[n + 1])
            rows = jnp.where(sub < count - 8 * n, rows, 0.0)
            main.append(rows[:, 0:128])
            third.append(rows[:, 128:256])
        for part in range(2):
            first, size, at = PARTS[part]
            n0, n1 = first // 8, size // 8
            half = n1 // 2
            low = [jnp.where(left, third[n0 + n], third[n0 + half + n]) for n in range(half)]
            out_ref[j, at:at + size, :] = jnp.concatenate(main[n0:n0 + n1], 0)
            out_ref[j, at + size:at + size + size // 2, :] = jnp.concatenate(low, 0) if half > 1 else low[0]
        return start + count

    lax.fori_loop(0, COLS, one, jnp.int32(0))


def coeff_kernel(counts_ref, x_ref, out_ref, buf_ref):
    transpose_pair(x_ref, buf_ref)
    transpose_third(x_ref, buf_ref)
    write_slots(counts_ref, buf_ref, out_ref)


def alpha_kernel(counts_ref, blocks_ref, types_ref, x_ref, table_ref, out_ref, buf_ref, a_ref, hi_ref, lo_ref):
    transpose_pair(x_ref, buf_ref)
    transpose_third(x_ref, buf_ref)
    blocks = NA // BLK
    for b in range(blocks):
        hi, lo = split(buf_ref[BLK * b:BLK * b + BLK, :])
        for half in range(2):
            at = slice(128 * b + BLK * half, 128 * b + BLK * half + BLK)
            hi_ref[at, :] = hi
            lo_ref[at, :] = lo

    def place(i, carry):
        for k in range(blocks):
            col = pl.multiple_of(blocks_ref[i, k] * 128, 128)
            row = pl.multiple_of(i * BLK, BLK)
            a_ref[pl.ds(row, BLK), pl.ds(col, 128)] = table_ref[types_ref[i, k]]
        return carry

    lax.fori_loop(0, blocks, place, 0)
    for r in range(4):
        rows = slice(256 * r, 256 * r + 256)
        a = a_ref[rows, :]
        buf_ref[rows, :] = jnp.dot(a, hi_ref[...], preferred_element_type=f32) + jnp.dot(
            a, lo_ref[...], preferred_element_type=f32
        )
    write_slots(counts_ref, buf_ref, out_ref)


def swap(x):
    return pltpu.roll(x, BLK, 1)


def fields(ref, j, size, at):
    main = ref[j, at:at + size, :]
    low = ref[j, at + size:at + size + size // 2, :]
    return main, swap(main), low, swap(low)


def unpack(ref, size, at, z_ref, base):
    left = left_half((size, 128))
    left_low = left_half((size // 2, 128))

    def one(j, carry):
        main, main_r, low, low_r = fields(ref, j, size, at)
        parts = (
            jnp.where(left, main, main_r),
            jnp.where(left, main_r, main),
            jnp.concatenate([jnp.where(left_low, low, low_r), jnp.where(left_low, low_r, low)], 0),
        )
        for n in range(3):
            hi, lo = split(parts[n])
            z_ref[base + 3 * j + n] = jnp.concatenate([hi, lo], 1)
        return carry

    lax.fori_loop(0, COLS, one, 0, unroll=2)


def own_kernel(own_ref, za_hbm, zb_hbm, za_ref, zb_ref, sems):
    copies = []
    for n, (z_ref, z_hbm) in enumerate(((za_ref, za_hbm), (zb_ref, zb_hbm))):
        _, size, at = PARTS[n]
        unpack(own_ref, size, at, z_ref, 0)
        copies.append(pltpu.make_async_copy(z_ref, z_hbm, sems.at[n]))
        copies[n].start()
    for copy in copies:
        copy.wait()


def product(blocks_ref, types_ref, z_ref, table_ref, size, trip_pairs, store, before=None, after=None):
    pick = left_half((size, 256)) | (lax.broadcasted_iota(jnp.int32, (size, 256), 1) // BLK == 2)
    left = left_half((size, 128))

    def block(m):
        hi, lo, w = [], [], []
        for k in range(0, DEPTH, 2):
            pair = jnp.where(pick, z_ref[blocks_ref[k, m]], z_ref[blocks_ref[k + 1, m]])
            hi.append(pair[:, 0:128])
            lo.append(pair[:, 128:256])
            w.append(table_ref[types_ref[k, m]])
            w.append(table_ref[types_ref[k + 1, m]])
        lhs = jnp.concatenate([jnp.concatenate(hi, 1), jnp.concatenate(lo, 1)], 0)
        both = jnp.dot(lhs, jnp.concatenate(w, 0), preferred_element_type=f32)
        both = both[0:size] + both[size:]
        return both + swap(both)

    def trip(n, carry):
        for i in range(trip_pairs):
            p = n * trip_pairs + i
            col = pl.ds(pl.multiple_of(p * 128, 128), 128)
            store(p, i % 3, col, jnp.where(left, block(2 * p), block(2 * p + 1)))
        return carry

    if before is None:
        lax.fori_loop(0, BLOCKS // (2 * trip_pairs), trip, 0)
        return
    for n in range(BLOCKS // (2 * trip_pairs)):
        before(n)
        trip(n, 0)
        after(n)


def first_kernel(blocks_ref, types_ref, own_hbm, partner_ref, table_ref, out_ref, z_ref, sem):
    size = PARTS[0][1]
    own_copy = pltpu.make_async_copy(own_hbm, z_ref.at[0:BLOCKS], sem)
    own_copy.start()
    unpack(partner_ref, size, 0, z_ref, BLOCKS)
    own_copy.wait()

    def store(p, kind, col, value):
        out_ref[:, col] = value

    product(blocks_ref, types_ref, z_ref, table_ref, size, 8 * TRIP, store)


def alpha_tile(alpha_ref, u, kind, length, at):
    left = left_half((length, 128))
    if kind == 0:
        return alpha_ref[2 * u, at:at + length, :]
    main = swap(alpha_ref[2 * u + 1, at:at + length, :])
    low_rows = slice(at + length, at + length + length // 2)
    if kind == 1:
        low = alpha_ref[2 * u, low_rows, :]
        return jnp.where(left, jnp.concatenate([low, swap(low)], 0), main)
    low = alpha_ref[2 * u + 1, low_rows, :]
    return jnp.where(left, main, jnp.concatenate([swap(low), low], 0))


def last_kernel(
    blocks_ref, types_ref, own_ref, partner_ref, table_ref, first_ref, alpha_hbm, out_hbm,
    z_ref, alpha_ref, out_ref, sem, alpha_sem, out_sems,
):
    (_, size_a, at_a), (start, size, at_b) = PARTS
    own_copy = pltpu.make_async_copy(own_ref, z_ref.at[0:BLOCKS], sem)
    own_copy.start()
    pieces = [slice(TRIP * 128 * n, TRIP * 128 * (n + 1)) for n in range(BLOCKS // (2 * TRIP))]
    stores = []
    alpha_copy = pltpu.make_async_copy(alpha_hbm, alpha_ref, alpha_sem)
    alpha_copy.start()
    unpack(partner_ref, size, 0, z_ref, BLOCKS)
    own_copy.wait()

    def store(p, kind, col, value):
        u = p // 3
        out_ref[0:start, col] = alpha_tile(alpha_ref, u, kind, size_a, at_a) + first_ref[:, col]
        out_ref[start:CAP, col] = alpha_tile(alpha_ref, u, kind, size, at_b) + value

    def before(n):
        if n == 0:
            alpha_copy.wait()

    def after(n):
        stores.append(pltpu.make_async_copy(out_ref.at[:, pieces[n]], out_hbm.at[:, pieces[n]], out_sems.at[n]))
        stores[n].start()

    product(blocks_ref, types_ref, z_ref, table_ref, size, TRIP, store, before, after)
    for copy in stores:
        copy.wait()


def grant(mib, **kw):
    return pltpu.CompilerParams(vmem_limit_bytes=mib << 20, **kw)


def in_vmem(x):
    return pltpu.with_memory_space_constraint(x, pltpu.VMEM)


def smem():
    return pl.BlockSpec(memory_space=pltpu.SMEM)


def vmem():
    return pl.BlockSpec(memory_space=pltpu.VMEM)


def hbm():
    return pl.BlockSpec(memory_space=pl.ANY)


def split_table(table):
    tiles = table.reshape(table.shape[0], BLK, BLK)
    hi = lax.reduce_precision(tiles, 8, 7)
    return jnp.concatenate([hi, tiles - hi], 2).astype(bf16)


def on_device(coeffs_t, alpha_table, alpha_blocks, alpha_types, beta_table, beta_blocks, beta_types, row_counts):
    slots = jax.ShapeDtypeStruct((COLS, PACK, 128), f32)
    coeff_slots = pl.pallas_call(
        coeff_kernel,
        in_specs=[smem(), vmem()],
        out_specs=vmem(),
        out_shape=slots,
        scratch_shapes=[pltpu.VMEM((ROWS, 256), f32)],
        name="coeff_slots",
    )(row_counts, coeffs_t)
    coeff_slots, alpha_table, beta_table = lax.optimization_barrier((coeff_slots, alpha_table, beta_table))
    alpha_slots = pl.pallas_call(
        alpha_kernel,
        in_specs=[smem(), smem(), smem(), vmem(), vmem()],
        out_specs=vmem(),
        out_shape=slots,
        scratch_shapes=[
            pltpu.VMEM((ROWS, 256), f32),
            pltpu.VMEM((NA, 2 * NA), bf16),
            pltpu.VMEM((2 * NA, 256), bf16),
            pltpu.VMEM((2 * NA, 256), bf16),
        ],
        name="alpha_slots",
    )(row_counts, alpha_blocks, alpha_types, coeffs_t, split_table(alpha_table))
    own = lax.all_to_all(coeff_slots, "col", split_axis=0, concat_axis=0, tiled=True)
    own, alpha_slots = lax.optimization_barrier((own, alpha_slots))
    route = [(i, i ^ 1) for i in range(8)]
    partner_first = lax.ppermute(own[:, :SPLIT], "cls", route)
    alpha = lax.all_to_all(alpha_slots, "col", split_axis=0, concat_axis=0, tiled=True)
    sizes = [PARTS[0][1], PARTS[1][1]]
    own_first, own_last = pl.pallas_call(
        own_kernel,
        in_specs=[vmem()],
        out_specs=[hbm(), hbm()],
        out_shape=[jax.ShapeDtypeStruct((BLOCKS, size, 256), bf16) for size in sizes],
        scratch_shapes=[pltpu.VMEM((BLOCKS, size, 256), bf16) for size in sizes]
        + [pltpu.SemaphoreType.DMA((2,))],
        name="own_split",
    )(in_vmem(own))
    rest, own_first, own_last, beta_table = lax.optimization_barrier(
        (own[:, SPLIT:], own_first, own_last, beta_table)
    )
    tiles = split_table(beta_table)
    partner_last = lax.ppermute(rest, "cls", route)
    blocks, types = beta_blocks.T, beta_types.T
    first = pl.pallas_call(
        first_kernel,
        in_specs=[smem(), smem(), hbm(), vmem(), vmem()],
        out_specs=vmem(),
        out_shape=jax.ShapeDtypeStruct((sizes[0], BLOCKS * BLK), f32),
        scratch_shapes=[
            pltpu.VMEM((2 * BLOCKS, sizes[0], 256), bf16),
            pltpu.SemaphoreType.DMA,
        ],
        compiler_params=grant(24),
        name="beta_first",
    )(blocks, types, own_first, in_vmem(partner_first), in_vmem(tiles))
    return pl.pallas_call(
        last_kernel,
        in_specs=[smem(), smem(), hbm(), vmem(), vmem(), vmem(), hbm()],
        out_specs=hbm(),
        out_shape=jax.ShapeDtypeStruct((CAP, BLOCKS * BLK), f32),
        scratch_shapes=[
            pltpu.VMEM((2 * BLOCKS, sizes[1], 256), bf16),
            pltpu.VMEM((COLS, PACK, 128), f32),
            pltpu.VMEM((CAP, BLOCKS * BLK), f32),
            pltpu.SemaphoreType.DMA,
            pltpu.SemaphoreType.DMA,
            pltpu.SemaphoreType.DMA((BLOCKS // (2 * TRIP),)),
        ],
        name="beta_last",
    )(blocks, types, own_last, in_vmem(partner_last), in_vmem(tiles), in_vmem(first), alpha)


def solution(mesh):
    return jax.shard_map(
        on_device,
        mesh=mesh,
        in_specs=(P(("cls", "col"), None), P(), P(), P(), P(), P("cls", None), P("cls", None), P()),
        out_specs=P("col", "cls"),
        check_vma=False,
    )
```
